32 devices in a mesh: rep: 8 (over z, y), fsdp: 4 (over x, core).
Axes of the slice: x: 2, y: 2, z: 4, core: 2. Of those that a mesh axis runs over, the one named last changes fastest.
Arguments:
- tokens: bfloat16 [4096, 576], P(('rep', 'fsdp')), may hold values from -6 to 6
- positions: int32 [4096], P(('rep', 'fsdp')), may hold values from 0 to 1212, as said below
- seq_count: int32 [32], P(('rep', 'fsdp')), may hold values from 0 to 2, as said below
- w_query: bfloat16 [1, 576, 576], P(None, 'fsdp'), may hold values from -0.25 to 0.25
- w_keyval: bfloat16 [1, 576, 384], P(None, 'fsdp'), may hold values from -0.25 to 0.25
- w_out: bfloat16 [1, 576, 576], P(None, 'fsdp'), may hold values from -0.75 to 0.75
- w_gateup: bfloat16 [1, 576, 3072], P(None, 'fsdp'), may hold values from -0.25 to 0.25
- w_down: bfloat16 [1, 1536, 576], P(None, 'fsdp'), may hold values from -0.15625 to 0.15625
- gain_attn: bfloat16 [1, 576], P(None, 'fsdp'), may hold values from 0.099609375 to 1.8984375
- gain_mlp: bfloat16 [1, 576], P(None, 'fsdp'), may hold values from 0.099609375 to 1.8984375
- out_grad: bfloat16 [4096, 576], P(('rep', 'fsdp')), may hold values from -6 to 6
Outputs:
- out_act: float32 [4096, 576], P(('rep', 'fsdp'))
- in_grad: float32 [4096, 576], P(('rep', 'fsdp'))
- grad_query: float32 [1, 576, 576], P(None, 'fsdp')
- grad_keyval: float32 [1, 576, 384], P(None, 'fsdp')
- grad_out: float32 [1, 576, 576], P(None, 'fsdp')
- grad_gateup: float32 [1, 576, 3072], P(None, 'fsdp')
- grad_down: float32 [1, 1536, 576], P(None, 'fsdp')
- grad_gain_attn: float32 [1, 576], P(None, 'fsdp')
- grad_gain_mlp: float32 [1, 576], P(None, 'fsdp')
The draws below stay inside these ranges and needn't reach their ends.
Inputs may be any that keep to these rules, and one draw needn't show every extreme that they name: Device d (rep index times 4 plus fsdp index) holds live sequences in its first seq_count[d] slots; the others hold data that no output may use. Some device fills all 2 slots. Within a sequence the positions rise by 1 to 3 from one token to the next; some sequence reaches the most.
All inputs are finite; a program needn't handle non-finite values.
Results may differ from the reference program's by a relative error of at most 0.015.
Values may be sent and summed in bfloat16 or wider, within the bound.
No kernel may reach another device: no remote copies, remote signals or barrier semaphores. Data moves between devices by JAX's collectives and lax.ppermute only.
A program may use at most 128 MiB of HBM per device.

```python
import jax
import jax.numpy as jnp
from jax import lax

D = 576
HEADS = 9
KVH = 3
HD = 64
FF = 1536
LAYERS = 1
CAP = 2
LEN = 64
DEVS = 32
SLOTS = 64
TOKENS = 4096
N_REP = 8
N_FSDP = 4


def draw_seq_count(key, part):
    base_count = jax.random.randint(jax.random.fold_in(key, 11), (DEVS,), 0, CAP + 1)
    chosen = jax.random.randint(jax.random.fold_in(key, 12), (), 0, DEVS)
    return jnp.where(jnp.arange(DEVS) == chosen, CAP, base_count).astype(jnp.int32)


def draw_positions(key, part):
    starts = jax.random.randint(jax.random.fold_in(key, 21), (SLOTS, 1), 0, 1024)
    steps_between = jax.random.randint(jax.random.fold_in(key, 22), (SLOTS, LEN), 1, 4)
    chosen = jax.random.randint(jax.random.fold_in(key, 23), (), 0, SLOTS)
    is_chosen = (jnp.arange(SLOTS) == chosen)[:, None]
    starts = jnp.where(is_chosen, 1023, starts)
    steps_between = jnp.where(is_chosen, 3, steps_between)
    rising = jnp.cumsum(steps_between, axis=1) - steps_between[:, :1]
    return (starts + rising).reshape(TOKENS).astype(jnp.int32)


def level_of(own_key, shape, cuts, low, top_value):
    loudness = 1.0
    for dim, shards_of in cuts:
        steps = jax.random.uniform(jax.random.fold_in(jax.random.fold_in(own_key, 6), dim), (shards_of,), jnp.float32, low / len(cuts), top_value / len(cuts))
        loudness = loudness * jnp.repeat(jnp.exp(steps), shape[dim] // shards_of).reshape((-1,) + (1,) * (len(shape) - 1 - dim))
    return loudness


def centred(rng, shape, scale, most, pieces=(), held_as=jnp.bfloat16):
    array = scale * jax.random.normal(rng, shape, jnp.float32)
    if pieces:
        array = array * level_of(rng, shape, pieces, -0.22, 0.18)
    return jnp.clip(array, -most, most).astype(held_as)


def setup_inputs(seed: int = 0) -> dict:
    key_list = jax.random.split(jax.random.key(seed), 12)
    return {
        "tokens": centred(key_list[0], (TOKENS, D), 1.0, 6.0, ((0, 32),)),
        "positions": draw_positions(jax.random.fold_in(key_list[11], 71), 0),
        "seq_count": draw_seq_count(jax.random.fold_in(key_list[11], 71), 0),
        "w_query": centred(key_list[3], (LAYERS, D, D), D ** -0.5, 0.25, ((1, 4),)),
        "w_keyval": centred(key_list[4], (LAYERS, D, 2 * KVH * HD), D ** -0.5, 0.25, ((1, 4),)),
        "w_out": centred(key_list[5], (LAYERS, D, D), (D // 8) ** -0.5, 0.75, ((1, 4),)),
        "w_gateup": centred(key_list[6], (LAYERS, D, 2 * FF), D ** -0.5, 0.25, ((1, 4),)),
        "w_down": centred(key_list[7], (LAYERS, FF, D), FF ** -0.5, 0.15625, ((1, 4),)),
        "gain_attn": jnp.clip(1.0 + 0.18 * jax.random.normal(key_list[8], (LAYERS, D), jnp.float32), 0.099609375, 1.8984375).astype(jnp.bfloat16),
        "gain_mlp": jnp.clip(1.0 + 0.18 * jax.random.normal(key_list[9], (LAYERS, D), jnp.float32), 0.099609375, 1.8984375).astype(jnp.bfloat16),
        "out_grad": centred(key_list[10], (TOKENS, D), 1.0, 6.0, ((0, 32),)),
    }


norm_eps = 1e-05
rope_base = 100000.0

@jax.custom_vjp
def low(v):
    return lax.optimization_barrier(v.astype(jnp.bfloat16)).astype(jnp.float32)

@jax.custom_vjp
def low_back(v):
    return v

def low_keep(v):
    return (low(v), None)

def low_pass(kept, grad):
    return (grad,)

def back_keep(v):
    return (v, None)

def back_low(kept, grad):
    return (low(grad),)
low.defvjp(low_keep, low_pass)
low_back.defvjp(back_keep, back_low)

def product(left_side, right_side):
    return jnp.dot(left_side, right_side, precision=lax.Precision.HIGHEST, preferred_element_type=jnp.float32)

def rms_scale(stream, gain_row):
    return stream * lax.rsqrt(lax.optimization_barrier(jnp.mean(stream * stream, axis=-1, keepdims=True)) + norm_eps) * gain_row

def rope_tables(positions):
    half_size = HD // 2
    frequency = rope_base ** (-(jnp.arange(half_size, dtype=jnp.float32) * 2.0 / HD))
    angle_table = positions.astype(jnp.float32)[..., None] * frequency
    angle_table = jnp.concatenate([angle_table, angle_table], axis=-1)[:, :, None, :]
    return (jnp.cos(angle_table), jnp.sin(angle_table))

def rotate(values, cosine, sine_table):
    half_size = values.shape[-1] // 2
    turned = jnp.concatenate([-values[..., half_size:], values[..., :half_size]], axis=-1)
    return values * cosine + turned * sine_table

def layer_forward(stream, cosine, sine_table, causal, w_query, w_keyval, w_out, w_gateup, w_down, gain_attn, gain_mlp):
    seq_total, seq_len, model_width = stream.shape
    kv_width = KVH * HD
    normed = low(rms_scale(stream, gain_attn))
    query_raw = low_back(product(normed, w_query)).reshape(seq_total, seq_len, HEADS, HD)
    keyval = low_back(product(normed, w_keyval))
    key_raw = keyval[..., :kv_width].reshape(seq_total, seq_len, KVH, HD)
    value_part = low(keyval[..., kv_width:]).reshape(seq_total, seq_len, KVH, HD)
    query_rot = low(rotate(query_raw, cosine, sine_table)).reshape(seq_total, seq_len, KVH, HEADS // KVH, HD)
    key_rot = low(rotate(key_raw, cosine, sine_table))
    scores = jnp.einsum('sqkgd,spkd->skgqp', query_rot, key_rot, precision=lax.Precision.HIGHEST) * HD ** (-0.5)
    scores = low_back(jnp.where(causal, scores, -1e+30))
    probs = low(jax.nn.softmax(scores, axis=-1))
    mixed_out = jnp.einsum('skgqp,spkd->sqkgd', probs, value_part, precision=lax.Precision.HIGHEST)
    mixed_out = low(low_back(mixed_out.reshape(seq_total, seq_len, model_width)))
    stream_mid = stream + low_back(product(mixed_out, w_out))
    normed_mid = low(rms_scale(stream_mid, gain_mlp))
    gateup = low_back(product(normed_mid, w_gateup))
    hidden = low(jax.nn.silu(gateup[..., :FF]) * gateup[..., FF:])
    return stream_mid + low_back(product(hidden, w_down))

def add_pair(first_term, second_term):
    return first_term + second_term

def reference(tokens, positions, seq_count, w_query, w_keyval, w_out, w_gateup, w_down, gain_attn, gain_mlp, out_grad):
    device_total = N_REP * N_FSDP
    slot_total = device_total * CAP
    live_rows = (jnp.arange(CAP, dtype=jnp.int32)[None, :] < seq_count[:, None]).reshape(slot_total)
    live_rows = live_rows.astype(jnp.float32)
    weights = tuple((weight.astype(jnp.float32) for weight in (w_query, w_keyval, w_out, w_gateup, w_down, gain_attn, gain_mlp)))
    per_step = N_FSDP * CAP
    tokens_in = tokens.astype(jnp.float32).reshape(-1, per_step, LEN, D)
    position_in = positions.reshape(-1, per_step, LEN)
    live_in = live_rows.reshape(-1, per_step, 1, 1)
    cotangent_in = out_grad.astype(jnp.float32).reshape(-1, per_step, LEN, D)
    causal = jnp.arange(LEN)[:, None] >= jnp.arange(LEN)[None, :]

    def step_fn(totals, step_input):
        stream_in, position_rows, live_mask, cotangent = step_input
        cosine, sine_table = rope_tables(position_rows)

        def forward(stream, weight_tuple):
            for layer_index in range(LAYERS):
                stream = layer_forward(stream, cosine, sine_table, causal, *(weight[layer_index] for weight in weight_tuple))
            return stream * live_mask
        result, pullback = jax.vjp(forward, stream_in, weights)
        grad_in, weight_grads = pullback(cotangent)
        return (jax.tree.map(add_pair, totals, weight_grads), (result, grad_in))
    zero_grads = jax.tree.map(jnp.zeros_like, weights)
    totals, (results, grads_in) = lax.scan(step_fn, zero_grads, (tokens_in, position_in, live_in, cotangent_in))
    out_act = results.reshape(-1, D)
    in_grad = grads_in.reshape(-1, D)
    return (out_act, in_grad, totals[0], totals[1], totals[2], totals[3], totals[4], totals[5], totals[6])
```

```python
import functools

import jax
import jax.numpy as jnp
from jax import lax
from jax.experimental import pallas as pl
from jax.experimental.pallas import tpu as pltpu
from jax.sharding import PartitionSpec as P

HEADS = 9
KVH = 3
HD = 64
LEN = 64
norm_eps = 1e-05
rope_base = 100000.0

BLOCK = 128
PAIRS = 5
QW = PAIRS * 128
F32 = jnp.float32
BF16 = jnp.bfloat16


def mm(left, right):
    return jnp.dot(left, right, preferred_element_type=F32)


def mm_nt(left, right):
    return lax.dot_general(left, right, (((1,), (1,)), ((), ())), preferred_element_type=F32)


def mm_tn(left, right):
    return lax.dot_general(left, right, (((0,), (0,)), ((), ())), preferred_element_type=F32)


def inverse_rms(stream):
    return lax.rsqrt(jnp.mean(stream * stream, axis=-1, keepdims=True) + norm_eps)


def lane_index(shape):
    return lax.broadcasted_iota(jnp.int32, shape, 1)


def own_columns(shard, rows, width):
    row = lax.broadcasted_iota(jnp.int32, (rows, width), 0)
    column = lax.broadcasted_iota(jnp.int32, (rows, width), 1)
    return (row == column + shard * width).astype(BF16)


def swapped(values, first_half):
    return jnp.where(first_half, pltpu.roll(values, 96, 1), pltpu.roll(values, 32, 1))


def split_heads(keyval):
    low = lane_index((BLOCK, 128)) < HD
    slices = [keyval[:, 128 * part : 128 * part + 128].astype(F32) for part in range(3)]

    def pair(piece, is_low):
        kept = jnp.where(low, piece, 0.0) if is_low else jnp.where(low, 0.0, piece)
        moved = pltpu.roll(kept, HD, 1)
        kept, moved = kept.astype(BF16), moved.astype(BF16)
        return (kept, moved) if is_low else (moved, kept)

    keys = [pair(slices[0], True), pair(slices[0], False), pair(slices[1], True)]
    values = [pair(slices[1], False), pair(slices[2], True), pair(slices[2], False)]
    return keys, values


def pair_operand(parts, pair):
    first = parts[(2 * pair) * KVH // HEADS][0]
    if 2 * pair + 1 >= HEADS:
        return first
    return jnp.concatenate([first, parts[(2 * pair + 1) * KVH // HEADS][1]], axis=0)


def attention_mask():
    query = lax.broadcasted_iota(jnp.int32, (BLOCK, BLOCK), 0)
    key = lax.broadcasted_iota(jnp.int32, (BLOCK, BLOCK), 1)
    return (query // LEN == key // LEN) & (query >= key)


def soft_rows(scores, allowed):
    halves = []
    for start in range(0, scores.shape[1], BLOCK):
        part = jnp.where(allowed, scores[:, start : start + BLOCK] * HD ** (-0.5), -1e30)
        part = jnp.exp(part - jnp.max(part, axis=-1, keepdims=True))
        halves.append(part / jnp.sum(part, axis=-1, keepdims=True))
    return halves


def joined(halves):
    return halves[0] if len(halves) == 1 else jnp.concatenate(halves, axis=1)


def attn_forward_kernel(n_shard, idx, *refs):
    tok = refs[:n_shard]
    small = refs[n_shard : 2 * n_shard]
    wq = refs[2 * n_shard : 3 * n_shard]
    wkv = refs[3 * n_shard : 4 * n_shard]
    wo = refs[4 * n_shard : 5 * n_shard]
    (x_ref, nrm_ref, q_ref, kv_ref, mix_ref, mid_ref, nmid_ref, cos_ref, sin_ref, gain_ref,
     wq_full, wkv_full, wo_full) = refs[5 * n_shard :]
    shard = idx[0]
    width = wq[0].shape[0]
    model = x_ref.shape[1]
    wq_full[:, model:] = jnp.zeros((model, QW - model), BF16)
    wo_full[model:, :] = jnp.zeros((QW - model, model), BF16)
    gains = jnp.zeros((16, model), F32)
    for part in range(n_shard):
        at = pl.multiple_of((shard ^ part) * width, 16)
        wq_full[pl.ds(at, width), :model] = wq[part][...]
        wkv_full[pl.ds(at, width), :] = wkv[part][...]
        wo_full[pl.ds(at, width), :] = wo[part][...]
        row = lax.broadcasted_iota(jnp.int32, (256, model), 0)
        column = lax.broadcasted_iota(jnp.int32, (256, model), 1)
        place = ((column == row + at) & (row < width)).astype(BF16)
        gains = gains + mm(small[part][...], place)
    gain_ref[...] = gains
    half = HD // 2
    step = lax.broadcasted_iota(jnp.int32, (half, 1), 0).astype(F32)
    frequency = jnp.exp(step * (-2.0 / HD * jnp.log(F32(rope_base))))
    for part in range(n_shard):
        codes = small[part][...].astype(F32)
        position = codes[0:1, :BLOCK] * 64.0 + codes[1:2, :BLOCK]
        angle = frequency * position
        rows = pl.ds(part * BLOCK, BLOCK)
        cos_ref[rows, :] = jnp.concatenate([jnp.cos(angle)] * 4, axis=0).T
        sin_ref[rows, :] = jnp.concatenate([jnp.sin(angle)] * 4, axis=0).T
        x_ref[rows, :] = tok[part][...]
    allowed = attention_mask()
    lane = lane_index((BLOCK, 128))
    first_half = lane % HD < half
    gain_attn = gains[2:3, :]
    gain_mlp = gains[3:4, :]

    def body(block, carry):
        rows = pl.ds(pl.multiple_of(block * BLOCK, BLOCK), BLOCK)
        stream = x_ref[rows, :].astype(F32)
        normed = (stream * inverse_rms(stream) * gain_attn).astype(BF16)
        nrm_ref[rows, :] = normed
        cosine = cos_ref[rows, :]
        sine = sin_ref[rows, :]
        sine = jnp.where(first_half, -sine, sine)
        query_raw = mm(normed, wq_full[...])
        keyval = mm(normed, wkv_full[...])

        def rope(values):
            return values * cosine + swapped(values, first_half) * sine

        key_first = rope(keyval[:, :128])
        key_second = jnp.where(lane < HD, rope(keyval[:, 128:256]), keyval[:, 128:256])
        keyval = jnp.concatenate([key_first, key_second, keyval[:, 256:]], axis=1).astype(BF16)
        kv_ref[rows, :] = keyval
        keys, values = split_heads(keyval)
        mixed = []
        for pair in range(PAIRS):
            query = rope(query_raw[:, 128 * pair : 128 * pair + 128]).astype(BF16)
            q_ref[rows, 128 * pair : 128 * pair + 128] = query
            soft = soft_rows(mm_nt(query, pair_operand(keys, pair)), allowed)
            mixed.append(mm(joined(soft).astype(BF16), pair_operand(values, pair)).astype(BF16))
        mixed = jnp.concatenate(mixed, axis=1)
        mix_ref[rows, :] = mixed
        stream_mid = stream + mm(mixed, wo_full[...])
        mid_ref[rows, :] = stream_mid
        nmid_ref[rows, :] = (stream_mid * inverse_rms(stream_mid) * gain_mlp).astype(BF16)
        return carry

    lax.fori_loop(0, n_shard, body, 0)


def bit_reverse(value, total):
    result = jnp.zeros_like(value)
    bit = 1
    while bit < total:
        result = result * 2 + (value & 1)
        value = value >> 1
        bit *= 2
    return result


def mlp_kernel(n_shard, n_rep, idx, *refs):
    nmid_ref, mid_ref, live_ref = refs[:3]
    cot = refs[3 : 3 + n_shard]
    wgu = refs[3 + n_shard : 3 + 2 * n_shard]
    wd = refs[3 + 2 * n_shard : 3 + 3 * n_shard]
    (act_ref, dn_ref, down_lo, down_hi, gu_lo, gu_hi, dcot_ref, w_full, down_all, gu_all) = refs[3 + 3 * n_shard :]
    shard = idx[0]
    member = idx[1]
    width = wgu[0].shape[0]
    ff = wgu[0].shape[1] // 2
    chunk = ff // n_shard
    for part in range(n_shard):
        at = pl.multiple_of((shard ^ part) * width, 16)
        w_full[pl.ds(at, width), :] = wgu[part][...]
        dcot_ref[pl.ds(part * BLOCK, BLOCK), :] = cot[part][...]
    normed_mid = nmid_ref[...]
    own_mid = mm(normed_mid, own_columns(shard, normed_mid.shape[1], width)).astype(BF16)
    d_branch = dcot_ref[...]
    result = mid_ref[...]
    gu_rows = gu_all.shape[1]
    groups = width // gu_rows
    down_rows = down_all.shape[1]
    for part in range(n_shard):
        place = shard ^ part
        gate_at = pl.ds(pl.multiple_of(place * chunk, 128), chunk)
        up_at = pl.ds(pl.multiple_of(place * chunk + ff, 128), chunk)
        gate = mm(normed_mid, w_full[:, gate_at])
        up = mm(normed_mid, w_full[:, up_at])
        d_hidden = mm_nt(d_branch, wd[part][...])
        sigmoid = 1.0 / (1.0 + jnp.exp(-gate))
        silu = gate * sigmoid
        hidden = (silu * up).astype(BF16)
        d_gate = (d_hidden * up * sigmoid * (1.0 + gate * (1.0 - sigmoid))).astype(BF16)
        d_up = (d_hidden * silu).astype(BF16)
        d_normed = mm_nt(d_gate, w_full[:, gate_at]) + mm_nt(d_up, w_full[:, up_at])
        if part == 0:
            dn_ref[...] = d_normed
            grad_down = mm_tn(hidden, d_branch)
            for slab in range(n_rep):
                to = bit_reverse(member ^ slab, n_rep)
                down_all[to] = grad_down[slab * down_rows : (slab + 1) * down_rows].astype(BF16)
        else:
            dn_ref[...] += d_normed
        result = result + mm(hidden[:BLOCK], wd[part][...])
        for offset, piece in ((0, d_gate), (n_shard, d_up)):
            grad = mm_tn(own_mid, piece)
            for group in range(groups):
                to = bit_reverse(member ^ ((place + offset) * groups + group), n_rep)
                gu_all[to] = grad[group * gu_rows : (group + 1) * gu_rows].astype(BF16)
    act_ref[...] = result * live_ref[...]
    middle = n_rep // 2
    down_lo[...] = down_all[:middle]
    down_hi[...] = down_all[middle:]
    gu_lo[...] = gu_all[:middle]
    gu_hi[...] = gu_all[middle:]


def attn_backward_kernel(n_shard, n_rep, idx, x_ref, nrm_ref, q_ref, kv_ref, mix_ref, mid_ref, cos_ref, sin_ref,
                         gain_ref, wq_full, wkv_full, wo_full, dn_ref, dcot_ref,
                         din_ref, a_lo, a_hi, dattn_all, dq_all, dkv_all, a_all):
    shard = idx[0]
    member = idx[1]
    model = x_ref.shape[1]
    width = model // n_shard
    half = HD // 2
    allowed = attention_mask()
    lane = lane_index((BLOCK, 128))
    first_half = lane % HD < half
    low = lane < HD
    gain_attn = gain_ref[2:3, :]
    gain_mlp = gain_ref[3:4, :]

    def body(block, carry):
        sum_attn, sum_mlp = carry
        rows = pl.ds(pl.multiple_of(block * BLOCK, BLOCK), BLOCK)
        stream = x_ref[rows, :].astype(F32)
        stream_mid = mid_ref[rows, :]
        inv_mlp = inverse_rms(stream_mid)
        d_normed_mid = dn_ref[rows, :]
        sum_mlp = sum_mlp + jnp.sum(d_normed_mid * stream_mid * inv_mlp, axis=0, keepdims=True)
        scaled = d_normed_mid * gain_mlp
        d_mid = (
            dcot_ref[rows, :].astype(F32)
            + inv_mlp * scaled
            - inv_mlp**3 * stream_mid * jnp.mean(scaled * stream_mid, axis=-1, keepdims=True)
        )
        d_attn = d_mid.astype(BF16)
        dattn_all[rows, :] = d_attn
        d_mixed = mm_nt(d_attn, wo_full[...]).astype(BF16)
        cosine = cos_ref[rows, :]
        sine = sin_ref[rows, :]
        sine = jnp.where(first_half, sine, -sine)

        def rope_back(grad):
            return grad * cosine + swapped(grad, first_half) * sine

        keyval = kv_ref[rows, :]
        keys, values = split_heads(keyval)
        d_keys = [[None, None] for _ in range(KVH)]
        d_values = [[None, None] for _ in range(KVH)]
        d_query = []

        def add_to(store, head, side, piece):
            held = store[head * KVH // HEADS][side]
            store[head * KVH // HEADS][side] = piece if held is None else held + piece

        for pair in range(PAIRS):
            columns = slice(128 * pair, 128 * pair + 128)
            query = q_ref[rows, columns]
            key_pair = pair_operand(keys, pair)
            d_mixed_pair = d_mixed[:, columns]
            soft = soft_rows(mm_nt(query, key_pair), allowed)
            d_probs = mm_nt(d_mixed_pair, pair_operand(values, pair))
            probs = joined(soft).astype(BF16)
            d_scores = []
            for side, part in enumerate(soft):
                d_part = d_probs[:, side * BLOCK : (side + 1) * BLOCK]
                d_scores.append(part * (d_part - jnp.sum(d_part * part, axis=-1, keepdims=True)))
            d_scores = joined(d_scores).astype(BF16)
            d_query.append(rope_back(mm(d_scores, key_pair) * HD ** (-0.5)).astype(BF16))
            d_key_pair = mm_tn(d_scores, query)
            d_value_pair = mm_tn(probs, d_mixed_pair)
            for side in range(len(soft)):
                here = slice(side * BLOCK, (side + 1) * BLOCK)
                add_to(d_keys, 2 * pair + side, side, d_key_pair[here])
                add_to(d_values, 2 * pair + side, side, d_value_pair[here])
        d_query = jnp.concatenate(d_query, axis=1)

        def placed(pieces, to_low):
            low_piece, high_piece = pieces
            if to_low:
                total = jnp.where(low, low_piece, 0.0)
                return total if high_piece is None else total + jnp.where(low, pltpu.roll(high_piece, HD, 1), 0.0)
            total = jnp.where(low, 0.0, pltpu.roll(low_piece, HD, 1))
            return total if high_piece is None else total + jnp.where(low, 0.0, high_piece)

        scale = HD ** (-0.5)
        first = rope_back((placed(d_keys[0], True) + placed(d_keys[1], False)) * scale)
        second = rope_back(placed(d_keys[2], True) * scale) + placed(d_values[0], False)
        third = placed(d_values[1], True) + placed(d_values[2], False)
        d_keyval = jnp.concatenate([first, second, third], axis=1).astype(BF16)
        dq_all[rows, :] = d_query
        dkv_all[rows, :] = d_keyval
        d_normed = mm_nt(d_query, wq_full[...]) + mm_nt(d_keyval, wkv_full[...])
        inv_attn = inverse_rms(stream)
        sum_attn = sum_attn + jnp.sum(d_normed * stream * inv_attn, axis=0, keepdims=True)

        @pl.when(block == 0)
        def _():
            scaled_in = d_normed * gain_attn
            din_ref[...] = (
                d_mid
                + inv_attn * scaled_in
                - inv_attn**3 * stream * jnp.mean(scaled_in * stream, axis=-1, keepdims=True)
            )

        return (sum_attn, sum_mlp)

    zero = jnp.zeros((1, model), F32)
    sum_attn, sum_mlp = lax.fori_loop(0, n_shard, body, (zero, zero))
    chosen = own_columns(shard, model, width)
    own_normed = mm(nrm_ref[...], chosen).astype(BF16)
    own_mixed = mm(mix_ref[:, :model], chosen).astype(BF16)
    kv_width = dkv_all.shape[1]
    a_all[:width, :] = mm_tn(own_normed, dq_all[:, :model])
    a_all[width : 2 * width, :] = mm_tn(own_mixed, dattn_all[...])
    a_all[2 * width : 3 * width, :kv_width] = mm_tn(own_normed, dkv_all[...])
    a_all[2 * width : 3 * width, kv_width:] = jnp.zeros((width, model - kv_width), F32)
    tail = a_all.shape[0] - 3 * width
    row = lax.broadcasted_iota(jnp.int32, (tail, model), 0)
    a_all[3 * width :, :] = jnp.where(row == 0, sum_attn, jnp.where(row == 1, sum_mlp, 0.0))
    rows = a_all.shape[0] // n_rep
    middle = n_rep // 2
    for slab in range(n_rep):
        to = bit_reverse(member ^ slab, n_rep)
        piece = a_all[slab * rows : (slab + 1) * rows, :].astype(BF16)

        @pl.when(to < middle)
        def _():
            a_lo[to] = piece

        @pl.when(to >= middle)
        def _():
            a_hi[to - middle] = piece


def unpack_down_kernel(n_rep, idx, first, second, out_ref):
    member = idx[1]
    middle = n_rep // 2
    rows = first.shape[1]
    for slab in range(n_rep):
        at = bit_reverse(member ^ slab, n_rep)
        here = pl.ds(slab * rows, rows)

        @pl.when(at < middle)
        def _():
            out_ref[here, :] = first[at].astype(F32)

        @pl.when(at >= middle)
        def _():
            out_ref[here, :] = second[at - middle].astype(F32)


def unpack_gateup_kernel(n_rep, idx, first, second, out_ref):
    member = idx[1]
    middle = n_rep // 2
    rows, columns = first.shape[1:]
    groups = out_ref.shape[0] // rows
    for slab in range(n_rep):
        at = bit_reverse(member ^ slab, n_rep)
        down = pl.ds((slab % groups) * rows, rows)
        across = pl.ds((slab // groups) * columns, columns)

        @pl.when(at < middle)
        def _():
            out_ref[down, across] = first[at].astype(F32)

        @pl.when(at >= middle)
        def _():
            out_ref[down, across] = second[at - middle].astype(F32)


def unpack_attn_kernel(n_rep, idx, first, second, q_ref, kv_ref, o_ref, gain_ref, a_all):
    unpack_down_kernel(n_rep, idx, first, second, a_all)
    width = q_ref.shape[0]
    q_ref[...] = a_all[:width, :]
    o_ref[...] = a_all[width : 2 * width, :]
    kv_ref[...] = a_all[2 * width : 3 * width, : kv_ref.shape[1]]
    gain_ref[...] = a_all[3 * width : 3 * width + 8, :]


def call(body, operands, outs, scratch=(), flops=0, moved=0, exps=0):
    vmem = pl.BlockSpec(memory_space=pltpu.VMEM)
    return pl.pallas_call(
        body,
        out_shape=outs,
        in_specs=[pl.BlockSpec(memory_space=pltpu.SMEM)] + [vmem] * (len(operands) - 1),
        out_specs=jax.tree.map(lambda _: vmem, outs),
        scratch_shapes=list(scratch),
        compiler_params=pltpu.CompilerParams(vmem_limit_bytes=56 * 2**20),
        cost_estimate=pl.CostEstimate(flops=flops, bytes_accessed=moved, transcendentals=exps),
    )(*operands)


def shape(dims, dtype):
    return jax.ShapeDtypeStruct(dims, dtype)


def exchange(value, axis, total, mask):
    return lax.ppermute(value, axis, [(member, member ^ mask) for member in range(total)])


def gather_group(value, total):
    held = [value]
    pieces = {0: value}
    bit = total // 2
    while bit:
        for known in sorted(pieces):
            pieces[known | bit] = exchange(pieces[known], "fsdp", total, bit)
        bit //= 2
    return [pieces[part] for part in range(total)]


def sum_over_replicas(low, high, total):
    mask = 1
    while True:
        arrived = exchange(high, "rep", total, mask)
        summed = (low.astype(F32) + arrived.astype(F32)).astype(BF16)
        mask *= 2
        count = summed.shape[0]
        if count == 1:
            break
        low, high = summed[: count // 2], summed[count // 2 :]
    held = summed
    mask = total // 2
    while True:
        arrived = exchange(held, "rep", total, mask)
        mask //= 2
        if mask == 0:
            return held, arrived
        held = jnp.concatenate([held, arrived], axis=0)


def on_device(n_rep, n_shard, tokens, positions, seq_count, w_query, w_keyval, w_out, w_gateup, w_down, gain_attn,
              gain_mlp, out_grad):
    row_count, model = tokens.shape
    width = w_query.shape[1]
    ff = w_gateup.shape[2] // 2
    kv_width = w_keyval.shape[2]
    group_rows = n_shard * row_count
    shard = lax.axis_index("fsdp").astype(jnp.int32)
    member = lax.axis_index("rep").astype(jnp.int32)
    idx = jnp.stack([shard, member])
    live = (jnp.arange(row_count, dtype=jnp.int32) // LEN < seq_count[0]).astype(F32)[:, None]
    cotangent = (out_grad.astype(F32) * live).astype(BF16)
    codes = jnp.stack([positions // 64, positions % 64]).astype(BF16)
    small = jnp.concatenate(
        [
            jnp.pad(codes, ((0, 0), (0, 256 - row_count))),
            jnp.pad(jnp.concatenate([gain_attn, gain_mlp], axis=0), ((0, 0), (0, 256 - width))),
            jnp.zeros((12, 256), BF16),
        ],
        axis=0,
    )
    tok = gather_group(tokens, n_shard)
    small = gather_group(small, n_shard)
    wq = gather_group(w_query[0], n_shard)
    wkv = gather_group(w_keyval[0], n_shard)
    wo = gather_group(w_out[0], n_shard)
    wgu = gather_group(w_gateup[0], n_shard)
    cot = gather_group(cotangent, n_shard)
    wd = gather_group(w_down[0], n_shard)
    (x_all, normed, query, keyval, mixed, mid, normed_mid, cosine, sine, gains, wq_full, wkv_full, wo_full) = call(
        functools.partial(attn_forward_kernel, n_shard),
        [idx] + tok + small + wq + wkv + wo,
        (
            shape((group_rows, model), BF16),
            shape((group_rows, model), BF16),
            shape((group_rows, QW), BF16),
            shape((group_rows, kv_width), BF16),
            shape((group_rows, QW), BF16),
            shape((group_rows, model), F32),
            shape((group_rows, model), BF16),
            shape((group_rows, 128), F32),
            shape((group_rows, 128), F32),
            shape((16, model), F32),
            shape((model, QW), BF16),
            shape((model, kv_width), BF16),
            shape((QW, model), BF16),
        ),
        flops=2 * group_rows * model * (2 * model + kv_width + 2 * 256),
        moved=8 * 2**20,
        exps=group_rows * 128 * HEADS,
    )
    middle = n_rep // 2
    groups = max(1, n_rep // (2 * n_shard))
    gu_slab = (width // groups, ff // n_shard)
    down_slab = (w_down.shape[1] // n_rep, model)
    a_rows = 3 * width + 16
    a_slab = (a_rows // n_rep, model)
    out_act, d_normed_mid, down_lo, down_hi, gu_lo, gu_hi, dcot = call(
        functools.partial(mlp_kernel, n_shard, n_rep),
        [idx, normed_mid, mid[:row_count], live] + cot + wgu + wd,
        (
            shape((row_count, model), F32),
            shape((group_rows, model), F32),
            shape((middle,) + down_slab, BF16),
            shape((middle,) + down_slab, BF16),
            shape((middle,) + gu_slab, BF16),
            shape((middle,) + gu_slab, BF16),
            shape((group_rows, model), BF16),
        ),
        [
            pltpu.VMEM((model, 2 * ff), BF16),
            pltpu.VMEM((n_rep,) + down_slab, BF16),
            pltpu.VMEM((n_rep,) + gu_slab, BF16),
        ],
        flops=2 * group_rows * model * 10 * ff // 2,
        moved=12 * 2**20,
        exps=group_rows * ff,
    )
    down = sum_over_replicas(down_lo, down_hi, n_rep)
    gateup = sum_over_replicas(gu_lo, gu_hi, n_rep)
    in_grad, a_lo, a_hi = call(
        functools.partial(attn_backward_kernel, n_shard, n_rep),
        [idx, x_all, normed, query, keyval, mixed, mid, cosine, sine, gains, wq_full, wkv_full, wo_full,
         d_normed_mid, dcot],
        (
            shape((row_count, model), F32),
            shape((middle,) + a_slab, BF16),
            shape((middle,) + a_slab, BF16),
        ),
        [
            pltpu.VMEM((group_rows, model), BF16),
            pltpu.VMEM((group_rows, QW), BF16),
            pltpu.VMEM((group_rows, kv_width), BF16),
            pltpu.VMEM((a_rows, model), F32),
        ],
        flops=2 * group_rows * model * (3 * model + 2 * kv_width),
        moved=8 * 2**20,
        exps=group_rows * 128 * HEADS,
    )
    attn = sum_over_replicas(a_lo, a_hi, n_rep)
    grad_down = call(
        functools.partial(unpack_down_kernel, n_rep),
        [idx] + list(down),
        shape((w_down.shape[1], model), F32),
        moved=2 * 2**20,
    )
    grad_gateup = call(
        functools.partial(unpack_gateup_kernel, n_rep),
        [idx] + list(gateup),
        shape((width, 2 * ff), F32),
        moved=3 * 2**20,
    )
    grad_query, grad_keyval, grad_out, gain_rows = call(
        functools.partial(unpack_attn_kernel, n_rep),
        [idx] + list(attn),
        (
            shape((width, model), F32),
            shape((width, kv_width), F32),
            shape((width, model), F32),
            shape((8, model), F32),
        ),
        [pltpu.VMEM((a_rows, model), F32)],
        moved=2 * 2**20,
    )
    own_gains = lax.dynamic_slice(gain_rows, (0, shard * width), (2, width))
    return (
        out_act,
        in_grad,
        grad_query[None],
        grad_keyval[None],
        grad_out[None],
        grad_gateup[None],
        grad_down[None],
        own_gains[:1],
        own_gains[1:],
    )


def solution(mesh):
    placed = (
        P(("rep", "fsdp"), None),
        P(("rep", "fsdp")),
        P(("rep", "fsdp")),
        P(None, "fsdp", None),
        P(None, "fsdp", None),
        P(None, "fsdp", None),
        P(None, "fsdp", None),
        P(None, "fsdp", None),
        P(None, "fsdp"),
        P(None, "fsdp"),
        P(("rep", "fsdp"), None),
    )
    return jax.shard_map(
        functools.partial(on_device, mesh.shape["rep"], mesh.shape["fsdp"]),
        mesh=mesh,
        in_specs=placed,
        out_specs=(
            P(("rep", "fsdp"), None),
            P(("rep", "fsdp"), None),
            P(None, "fsdp", None),
            P(None, "fsdp", None),
            P(None, "fsdp", None),
            P(None, "fsdp", None),
            P(None, "fsdp", None),
            P(None, "fsdp"),
            P(None, "fsdp"),
        ),
        check_vma=False,
    )
```

```python
import functools

import jax
import jax.numpy as jnp
from jax import lax
from jax.experimental import pallas as pl
from jax.experimental.pallas import tpu as pltpu
from jax.sharding import PartitionSpec as P

HEADS = 9
KVH = 3
HD = 64
LEN = 64
norm_eps = 1e-05
rope_base = 100000.0

BLOCK = 128
PAIRS = 5
QW = PAIRS * 128
UNROLL = 4
MICROS = (7, 6, 6, 13)
F32 = jnp.float32
BF16 = jnp.bfloat16


def mm(left, right):
    return jnp.dot(left, right, preferred_element_type=F32)


def mm_nt(left, right):
    return lax.dot_general(left, right, (((1,), (1,)), ((), ())), preferred_element_type=F32)


def mm_tn(left, right):
    return lax.dot_general(left, right, (((0,), (0,)), ((), ())), preferred_element_type=F32)


def inverse_rms(stream):
    return lax.rsqrt(jnp.mean(stream * stream, axis=-1, keepdims=True) + norm_eps)


def lane_index(shape):
    return lax.broadcasted_iota(jnp.int32, shape, 1)


def own_columns(shard, rows, width):
    row = lax.broadcasted_iota(jnp.int32, (rows, width), 0)
    column = lax.broadcasted_iota(jnp.int32, (rows, width), 1)
    return (row == column + shard * width).astype(BF16)


def swapped(values, first_half):
    return jnp.where(first_half, pltpu.roll(values, 96, 1), pltpu.roll(values, 32, 1))


def split_heads(keyval):
    low = lane_index((BLOCK, 128)) < HD
    slices = [keyval[:, 128 * part : 128 * part + 128].astype(F32) for part in range(3)]

    def pair(piece, is_low):
        kept = jnp.where(low, piece, 0.0) if is_low else jnp.where(low, 0.0, piece)
        moved = pltpu.roll(kept, HD, 1)
        kept, moved = kept.astype(BF16), moved.astype(BF16)
        return (kept, moved) if is_low else (moved, kept)

    keys = [pair(slices[0], True), pair(slices[0], False), pair(slices[1], True)]
    values = [pair(slices[1], False), pair(slices[2], True), pair(slices[2], False)]
    return keys, values


def pair_operand(parts, pair):
    first = parts[(2 * pair) * KVH // HEADS][0]
    if 2 * pair + 1 >= HEADS:
        return first
    return jnp.concatenate([first, parts[(2 * pair + 1) * KVH // HEADS][1]], axis=0)


def attention_mask():
    query = lax.broadcasted_iota(jnp.int32, (BLOCK, BLOCK), 0)
    key = lax.broadcasted_iota(jnp.int32, (BLOCK, BLOCK), 1)
    return (query // LEN == key // LEN) & (query >= key)


def soft_rows(scores, allowed):
    halves = []
    for start in range(0, scores.shape[1], BLOCK):
        part = jnp.where(allowed, scores[:, start : start + BLOCK], -1e30)
        part = jnp.exp(part - jnp.max(part, axis=-1, keepdims=True))
        halves.append(part * (1.0 / jnp.sum(part, axis=-1, keepdims=True)))
    return halves


def joined(halves):
    return halves[0] if len(halves) == 1 else jnp.concatenate(halves, axis=1)


def attn_forward_kernel(n_shard, idx, *refs):
    tok = refs[:n_shard]
    small = refs[n_shard : 2 * n_shard]
    wq = refs[2 * n_shard : 3 * n_shard]
    wkv = refs[3 * n_shard : 4 * n_shard]
    wo = refs[4 * n_shard : 5 * n_shard]
    (x_ref, nrm_ref, q_ref, kv_ref, mix_ref, mid_ref, nmid_ref, cos_ref, sin_ref, gain_ref,
     wq_full, wkv_full, wo_full, query_all, keyval_all) = refs[5 * n_shard :]
    shard = idx[0]
    width = wq[0].shape[0]
    model = x_ref.shape[1]
    wq_full[:, model:] = jnp.zeros((model, QW - model), BF16)
    wo_full[model:, :] = jnp.zeros((QW - model, model), BF16)
    gains = jnp.zeros((16, model), F32)
    for part in range(n_shard):
        at = pl.multiple_of((shard ^ part) * width, 16)
        wq_full[pl.ds(at, width), :model] = wq[part][...]
        wkv_full[pl.ds(at, width), :] = wkv[part][...]
        wo_full[pl.ds(at, width), :] = wo[part][...]
        row = lax.broadcasted_iota(jnp.int32, (256, model), 0)
        column = lax.broadcasted_iota(jnp.int32, (256, model), 1)
        place = ((column == row + at) & (row < width)).astype(BF16)
        gains = gains + mm(small[part][...], place)
    gain_ref[...] = gains
    half = HD // 2
    step = lax.broadcasted_iota(jnp.int32, (half, 1), 0).astype(F32)
    frequency = jnp.exp(step * (-2.0 / HD * jnp.log(F32(rope_base))))
    for part in range(n_shard):
        codes = small[part][...].astype(F32)
        position = codes[0:1, :BLOCK] * 64.0 + codes[1:2, :BLOCK]
        angle = frequency * position
        rows = pl.ds(part * BLOCK, BLOCK)
        cos_ref[rows, :] = jnp.concatenate([jnp.cos(angle)] * 4, axis=0).T
        sin_ref[rows, :] = jnp.concatenate([jnp.sin(angle)] * 4, axis=0).T
        x_ref[rows, :] = tok[part][...]
    allowed = attention_mask()
    lane = lane_index((BLOCK, 128))
    first_half = lane % HD < half
    gain_attn = gains[2:3, :]
    gain_mlp = gains[3:4, :]

    for part in range(n_shard):
        stream = tok[part][...].astype(F32)
        rows = pl.ds(part * BLOCK, BLOCK)
        nrm_ref[rows, :] = (stream * inverse_rms(stream) * gain_attn).astype(BF16)
    query_all[...] = mm(nrm_ref[...], wq_full[...])
    keyval_all[...] = mm(nrm_ref[...], wkv_full[...])

    def body(block, carry):
        rows = pl.ds(pl.multiple_of(block * BLOCK, BLOCK), BLOCK)
        cosine = cos_ref[rows, :]
        sine = sin_ref[rows, :]
        sine = jnp.where(first_half, -sine, sine)
        query_raw = query_all[rows, :]
        keyval = keyval_all[rows, :]

        def rope(values):
            return values * cosine + swapped(values, first_half) * sine

        key_first = rope(keyval[:, :128])
        key_second = jnp.where(lane < HD, rope(keyval[:, 128:256]), keyval[:, 128:256])
        keyval = jnp.concatenate([key_first, key_second, keyval[:, 256:]], axis=1).astype(BF16)
        kv_ref[rows, :] = keyval
        keys, values = split_heads(keyval)
        mixed = []
        for pair in range(PAIRS):
            query = (rope(query_raw[:, 128 * pair : 128 * pair + 128]) * HD ** (-0.5)).astype(BF16)
            q_ref[rows, 128 * pair : 128 * pair + 128] = query
            soft = soft_rows(mm_nt(query, pair_operand(keys, pair)), allowed)
            mixed.append(mm(joined(soft).astype(BF16), pair_operand(values, pair)).astype(BF16))
        mixed = jnp.concatenate(mixed, axis=1)
        mix_ref[rows, :] = mixed
        return carry

    lax.fori_loop(0, n_shard, body, 0, unroll=UNROLL)
    stream_mid = x_ref[...].astype(F32) + mm(mix_ref[...], wo_full[...])
    mid_ref[...] = stream_mid
    nmid_ref[...] = (stream_mid * inverse_rms(stream_mid) * gain_mlp).astype(BF16)


def bit_reverse(value, total):
    result = jnp.zeros_like(value)
    bit = 1
    while bit < total:
        result = result * 2 + (value & 1)
        value = value >> 1
        bit *= 2
    return result


def spread(target, member, n_rep, first_row, slab, value):
    to = bit_reverse(member ^ slab, n_rep)
    target[to, first_row : first_row + value.shape[0], :] = value.astype(BF16)


def mlp_kernel(n_shard, n_rep, first_call, idx, *refs):
    if first_call:
        (nmid_ref, mid_ref, wd_own, wd_other), cot, wgu = refs[:4], refs[4 : 4 + n_shard], refs[4 + n_shard : -13]
        (act_ref, dn_ref, lo_ref, hi_ref, dcot_ref, w_full, own_ref, all_ref, wd_pair, wide_ref, sem, wd_sem,
         cot_sem) = refs[-13:]
    else:
        (nmid_ref, act_in, live_ref, wd_own, wd_other, dcot_ref, w_full, own_ref, dn_in, act_ref, dn_ref, lo_ref,
         hi_ref, all_ref, wd_pair, wd_sem) = refs
    shard = idx[0]
    member = idx[1]
    first = 0 if first_call else 2
    model = nmid_ref.shape[1]
    ff = w_full.shape[1] // 2
    chunk = ff // n_shard
    waits = []
    for part, source in ((first, wd_own), (first + 1, wd_other)):
        at = pl.multiple_of(((shard ^ part) & 1) * chunk, 128)
        waits.append(pltpu.make_async_copy(source, wd_pair.at[pl.ds(at, chunk)], wd_sem.at[part - first]))
    if first_call:
        width = model // n_shard
        side = member & 1
        pieces = [(0, wgu[0], None), (1, wgu[1], None), (2, wgu[2], side), (2, wgu[3], 1 - side),
                  (3, wgu[4], side), (3, wgu[5], 1 - side)]
        for number, (part, source, which) in enumerate(pieces):
            down = pl.ds(pl.multiple_of((shard ^ part) * width, 16), width)
            if which is None:
                target = w_full.at[down]
            else:
                target = w_full.at[down, pl.ds(pl.multiple_of(which * ff, 128), ff)]
            waits.append(pltpu.make_async_copy(source, target, sem.at[number]))
        for part in range(n_shard):
            waits.append(
                pltpu.make_async_copy(cot[part], dcot_ref.at[pl.ds(part * BLOCK, BLOCK)], cot_sem.at[part])
            )
    for wait in waits:
        wait.start()
    if first_call:
        own_ref[...] = mm(nmid_ref[...], own_columns(shard, model, width)).astype(BF16)
    for wait in waits:
        wait.wait()
    normed_mid = nmid_ref[...]
    d_branch = dcot_ref[...]
    base = ((shard ^ first) >> 1) * 2 * chunk
    gate_at = pl.ds(pl.multiple_of(base, 256), 2 * chunk)
    up_at = pl.ds(pl.multiple_of(base + ff, 256), 2 * chunk)
    gate = mm(normed_mid, w_full[:, gate_at])
    up = mm(normed_mid, w_full[:, up_at])
    d_hidden = mm_nt(d_branch, wd_pair[...])
    sigmoid = 0.5 * jnp.tanh(0.5 * gate) + 0.5
    silu = gate * sigmoid
    hidden = (silu * up).astype(BF16)
    d_gate = (d_hidden * up * sigmoid * (1.0 + gate * (1.0 - sigmoid))).astype(BF16)
    d_up = (d_hidden * silu).astype(BF16)
    rows = all_ref.shape[1]
    if first_call:
        wide_ref[...] = hidden
        own_hidden = wide_ref[:, pl.ds(pl.multiple_of((shard & 1) * chunk, 128), chunk)]
        rows = rows // 2
        grad_down = mm_tn(own_hidden, d_branch)
        tail = grad_down[:, chunk:]
        half = chunk // 2
        grad_down = jnp.concatenate(
            [grad_down[:, :chunk], jnp.concatenate([tail[:half], tail[half:]], axis=1)], axis=0
        )
        for slab in range(n_rep):
            spread(all_ref, member, n_rep, rows, slab, grad_down[slab * rows : (slab + 1) * rows])
    slab = 0
    for piece in (d_gate, d_up):
        grad = mm_tn(own_ref[...], piece)
        for column in range(0, 2 * chunk, chunk):
            for row in range(0, grad.shape[0], rows):
                spread(all_ref, member, n_rep, 0, slab, grad[row : row + rows, column : column + chunk])
                slab += 1
    middle = n_rep // 2
    lo_ref[...] = all_ref[:middle]
    hi_ref[...] = all_ref[middle:]
    d_normed = mm_nt(d_gate, w_full[:, gate_at]) + mm_nt(d_up, w_full[:, up_at])
    added = mm(hidden[:BLOCK], wd_pair[...])
    if first_call:
        dn_ref[...] = d_normed
        act_ref[...] = mid_ref[:BLOCK, :] + added
    else:
        dn_ref[...] = dn_in[...] + d_normed
        act_ref[...] = (act_in[...] + added) * live_ref[...]


def attn_backward_kernel(n_shard, n_rep, idx, x_ref, nrm_ref, q_ref, kv_ref, mix_ref, mid_ref, cos_ref, sin_ref,
                         gain_ref, wq_full, wkv_full, wo_full, dn_ref, dcot_ref,
                         din_ref, a_lo, a_hi, dattn_all, dmix_all, dq_all, dkv_all, a_all):
    shard = idx[0]
    member = idx[1]
    model = x_ref.shape[1]
    width = model // n_shard
    half = HD // 2
    allowed = attention_mask()
    lane = lane_index((BLOCK, 128))
    first_half = lane % HD < half
    low = lane < HD
    gain_attn = gain_ref[2:3, :]
    gain_mlp = gain_ref[3:4, :]

    stream_mid = mid_ref[...]
    inv_mlp = inverse_rms(stream_mid)
    d_normed_mid = dn_ref[...]
    sum_mlp = jnp.sum(d_normed_mid * stream_mid * inv_mlp, axis=0, keepdims=True)
    scaled = d_normed_mid * gain_mlp
    d_mid = (
        dcot_ref[...].astype(F32)
        + inv_mlp * scaled
        - inv_mlp**3 * stream_mid * jnp.mean(scaled * stream_mid, axis=-1, keepdims=True)
    )
    din_ref[...] = d_mid[:BLOCK, :]
    dattn_all[...] = d_mid.astype(BF16)
    dmix_all[...] = mm_nt(dattn_all[...], wo_full[...]).astype(BF16)

    def body(block, carry):
        rows = pl.ds(pl.multiple_of(block * BLOCK, BLOCK), BLOCK)
        d_mixed = dmix_all[rows, :]
        cosine = cos_ref[rows, :]
        sine = sin_ref[rows, :]
        sine = jnp.where(first_half, sine, -sine)

        def rope_back(grad):
            return grad * cosine + swapped(grad, first_half) * sine

        keyval = kv_ref[rows, :]
        keys, values = split_heads(keyval)
        d_keys = [[None, None] for _ in range(KVH)]
        d_values = [[None, None] for _ in range(KVH)]
        d_query = []

        def add_to(store, head, side, piece):
            held = store[head * KVH // HEADS][side]
            store[head * KVH // HEADS][side] = piece if held is None else held + piece

        for pair in range(PAIRS):
            columns = slice(128 * pair, 128 * pair + 128)
            query = q_ref[rows, columns]
            key_pair = pair_operand(keys, pair)
            d_mixed_pair = d_mixed[:, columns]
            soft = soft_rows(mm_nt(query, key_pair), allowed)
            d_probs = mm_nt(d_mixed_pair, pair_operand(values, pair))
            probs = joined(soft).astype(BF16)
            d_scores = []
            for side, part in enumerate(soft):
                d_part = d_probs[:, side * BLOCK : (side + 1) * BLOCK]
                d_scores.append(part * (d_part - jnp.sum(d_part * part, axis=-1, keepdims=True)))
            d_scores = joined(d_scores).astype(BF16)
            d_query.append(rope_back(mm(d_scores, key_pair) * HD ** (-0.5)).astype(BF16))
            d_key_pair = mm_tn(d_scores, query)
            d_value_pair = mm_tn(probs, d_mixed_pair)
            for side in range(len(soft)):
                here = slice(side * BLOCK, (side + 1) * BLOCK)
                add_to(d_keys, 2 * pair + side, side, d_key_pair[here])
                add_to(d_values, 2 * pair + side, side, d_value_pair[here])
        d_query = jnp.concatenate(d_query, axis=1)

        def placed(pieces, to_low):
            low_piece, high_piece = pieces
            if to_low:
                total = jnp.where(low, low_piece, 0.0)
                return total if high_piece is None else total + jnp.where(low, pltpu.roll(high_piece, HD, 1), 0.0)
            total = jnp.where(low, 0.0, pltpu.roll(low_piece, HD, 1))
            return total if high_piece is None else total + jnp.where(low, 0.0, high_piece)

        first = rope_back(placed(d_keys[0], True) + placed(d_keys[1], False))
        second = rope_back(placed(d_keys[2], True)) + placed(d_values[0], False)
        third = placed(d_values[1], True) + placed(d_values[2], False)
        d_keyval = jnp.concatenate([first, second, third], axis=1).astype(BF16)
        dq_all[rows, :] = d_query
        dkv_all[rows, :] = d_keyval
        return carry

    lax.fori_loop(0, n_shard, body, 0, unroll=UNROLL)
    d_normed = mm_nt(dq_all[...], wq_full[...]) + mm_nt(dkv_all[...], wkv_full[...])
    stream = x_ref[...].astype(F32)
    inv_attn = inverse_rms(stream)
    sum_attn = jnp.sum(d_normed * stream * inv_attn, axis=0, keepdims=True)
    own_in = d_normed[:BLOCK, :] * gain_attn
    own_stream = stream[:BLOCK, :]
    own_inv = inv_attn[:BLOCK, :]
    din_ref[...] += own_inv * own_in - own_inv**3 * own_stream * jnp.mean(own_in * own_stream, axis=-1, keepdims=True)
    chosen = own_columns(shard, model, width)
    own_normed = mm(nrm_ref[...], chosen).astype(BF16)
    own_mixed = mm(mix_ref[:, :model], chosen).astype(BF16)
    kv_width = dkv_all.shape[1]
    a_all[:width, :] = mm_tn(own_normed, dq_all[:, :model])
    a_all[width : 2 * width, :] = mm_tn(own_mixed, dattn_all[...])
    a_all[2 * width : 3 * width, :kv_width] = mm_tn(own_normed, dkv_all[...])
    a_all[2 * width : 3 * width, kv_width:] = jnp.zeros((width, model - kv_width), F32)
    tail = a_all.shape[0] - 3 * width
    row = lax.broadcasted_iota(jnp.int32, (tail, model), 0)
    a_all[3 * width :, :] = jnp.where(row == 0, sum_attn, jnp.where(row == 1, sum_mlp, 0.0))
    rows = a_all.shape[0] // n_rep
    middle = n_rep // 2
    for slab in range(n_rep):
        to = bit_reverse(member ^ slab, n_rep)
        piece = a_all[slab * rows : (slab + 1) * rows, :].astype(BF16)

        @pl.when(to < middle)
        def _():
            a_lo[to] = piece

        @pl.when(to >= middle)
        def _():
            a_hi[to - middle] = piece


def fetch(first, second, member, slab, n_rep, target, rows):
    at = bit_reverse(member ^ slab, n_rep)
    middle = n_rep // 2

    @pl.when(at < middle)
    def _():
        target[pl.ds(slab * rows, rows), :] = first[at].astype(F32)

    @pl.when(at >= middle)
    def _():
        target[pl.ds(slab * rows, rows), :] = second[at - middle].astype(F32)


def unpack_mlp_kernel(n_rep, n_shard, idx, one_lo, one_hi, two_lo, two_hi, down_ref, gu_ref):
    shard = idx[0]
    member = idx[1]
    middle = n_rep // 2
    rows, chunk = two_lo.shape[1:]
    ff = gu_ref.shape[1] // 2
    half = chunk // 2
    groups = gu_ref.shape[0] // rows

    def place_down(slab, piece):
        row = slab * rows
        if row < chunk:
            count = min(rows, chunk - row)
            down_ref[row : row + count, :chunk] = piece[:count]
            piece = piece[count:]
            row += count
        if piece.shape[0]:
            row -= chunk
            down_ref[row : row + piece.shape[0], chunk:] = piece[:, :half]
            down_ref[half + row : half + row + piece.shape[0], chunk:] = piece[:, half:]

    def place_gateup(slab, pair, piece):
        up, rest = divmod(slab, 2 * groups)
        column, group = divmod(rest, groups)
        base = ((shard ^ (2 * pair)) >> 1) * 2 * chunk + column * chunk + up * ff
        gu_ref[group * rows : (group + 1) * rows, pl.ds(pl.multiple_of(base, 128), chunk)] = piece

    for slab in range(n_rep):
        at = bit_reverse(member ^ slab, n_rep)

        def place(one, two, where):
            piece = one[where].astype(F32)
            place_gateup(slab, 0, piece[:rows])
            place_down(slab, piece[rows:])
            place_gateup(slab, 1, two[where].astype(F32))

        @pl.when(at < middle)
        def _():
            place(one_lo, two_lo, at)

        @pl.when(at >= middle)
        def _():
            place(one_hi, two_hi, at - middle)


def unpack_attn_kernel(n_rep, idx, first, second, q_ref, kv_ref, o_ref, gain_ref, a_all):
    rows = first.shape[1]
    for slab in range(n_rep):
        fetch(first, second, idx[1], slab, n_rep, a_all, rows)
    width = q_ref.shape[0]
    q_ref[...] = a_all[:width, :]
    o_ref[...] = a_all[width : 2 * width, :]
    kv_ref[...] = a_all[2 * width : 3 * width, : kv_ref.shape[1]]
    gain_ref[...] = a_all[3 * width : 3 * width + 8, :]


def call(body, operands, outs, scratch=(), micros=1, vmem=24, raw=()):
    in_vmem = pl.BlockSpec(memory_space=pltpu.VMEM)
    in_hbm = pl.BlockSpec(memory_space=pltpu.HBM)
    specs = [in_hbm if number in raw else in_vmem for number in range(1, len(operands))]
    return pl.pallas_call(
        body,
        out_shape=outs,
        in_specs=[pl.BlockSpec(memory_space=pltpu.SMEM)] + specs,
        out_specs=jax.tree.map(lambda _: in_vmem, outs),
        scratch_shapes=list(scratch),
        compiler_params=pltpu.CompilerParams(vmem_limit_bytes=vmem * 2**20),
        cost_estimate=pl.CostEstimate(flops=int(micros * 1e9), bytes_accessed=2**20, transcendentals=0),
    )(*operands)


def shape(dims, dtype):
    return jax.ShapeDtypeStruct(dims, dtype)


def exchange(value, axis, total, mask):
    return lax.ppermute(value, axis, [(member, member ^ mask) for member in range(total)])


def gather_group(value, total):
    held = [value]
    pieces = {0: value}
    bit = total // 2
    while bit:
        for known in sorted(pieces):
            pieces[known | bit] = exchange(pieces[known], "fsdp", total, bit)
        bit //= 2
    return [pieces[part] for part in range(total)]


def sum_over_replicas(low, high, total):
    mask = 1
    while True:
        arrived = exchange(high, "rep", total, mask)
        summed = (low.astype(F32) + arrived.astype(F32)).astype(BF16)
        mask *= 2
        count = summed.shape[0]
        if count == 1:
            break
        low, high = summed[: count // 2], summed[count // 2 :]
    held = summed
    mask = total // 2
    while True:
        arrived = exchange(held, "rep", total, mask)
        mask //= 2
        if mask == 0:
            return held, arrived
        held = jnp.concatenate([held, arrived], axis=0)


def on_device(n_rep, n_shard, tokens, positions, seq_count, w_query, w_keyval, w_out, w_gateup, w_down, gain_attn,
              gain_mlp, out_grad):
    row_count, model = tokens.shape
    width = w_query.shape[1]
    ff = w_gateup.shape[2] // 2
    kv_width = w_keyval.shape[2]
    group_rows = n_shard * row_count
    shard = lax.axis_index("fsdp").astype(jnp.int32)
    member = lax.axis_index("rep").astype(jnp.int32)
    idx = jnp.stack([shard, member])
    live = (jnp.arange(row_count, dtype=jnp.int32) // LEN < seq_count[0]).astype(F32)[:, None]
    cotangent = (out_grad.astype(F32) * live).astype(BF16)
    codes = jnp.stack([positions // 64, positions % 64]).astype(BF16)
    small = jnp.concatenate(
        [
            jnp.pad(codes, ((0, 0), (0, 256 - row_count))),
            jnp.pad(jnp.concatenate([gain_attn, gain_mlp], axis=0), ((0, 0), (0, 256 - width))),
            jnp.zeros((12, 256), BF16),
        ],
        axis=0,
    )
    tok = gather_group(tokens, n_shard)
    small = gather_group(small, n_shard)
    wq = gather_group(w_query[0], n_shard)
    wkv = gather_group(w_keyval[0], n_shard)
    wo = gather_group(w_out[0], n_shard)
    side = member & 1
    gu_direct = exchange(lax.dynamic_slice(w_gateup[0], (0, side * ff), (width, ff)), "fsdp", n_shard, 2)
    gu_around = exchange(gu_direct, "rep", n_rep, 1)
    cot_across = exchange(cotangent, "fsdp", n_shard, 2)
    down_across = exchange(w_down[0], "fsdp", n_shard, 2)
    (x_all, normed, query, keyval, mixed, mid, normed_mid, cosine, sine, gains, wq_full, wkv_full, wo_full) = call(
        functools.partial(attn_forward_kernel, n_shard),
        [idx] + tok + small + wq + wkv + wo,
        (
            shape((group_rows, model), BF16),
            shape((group_rows, model), BF16),
            shape((group_rows, QW), BF16),
            shape((group_rows, kv_width), BF16),
            shape((group_rows, QW), BF16),
            shape((group_rows, model), F32),
            shape((group_rows, model), BF16),
            shape((group_rows, 128), F32),
            shape((group_rows, 128), F32),
            shape((16, model), F32),
            shape((model, QW), BF16),
            shape((model, kv_width), BF16),
            shape((QW, model), BF16),
        ),
        [pltpu.VMEM((group_rows, QW), F32), pltpu.VMEM((group_rows, kv_width), F32)],
        micros=MICROS[0],
    )
    middle = n_rep // 2
    chunk = ff // n_shard
    slab_rows = width * 4 // n_rep
    a_rows = 3 * width + 16
    a_slab = (a_rows // n_rep, model)
    gu_own, cot_own, down_own, gu_direct, gu_around, cot_across, down_across, _ = lax.optimization_barrier(
        (w_gateup[0], cotangent, w_down[0], gu_direct, gu_around, cot_across, down_across, gains)
    )
    gu = [gu_own, exchange(gu_own, "fsdp", n_shard, 1), gu_direct, gu_around,
          exchange(gu_direct, "fsdp", n_shard, 1), exchange(gu_around, "fsdp", n_shard, 1)]
    cot = [cot_own, exchange(cot_own, "fsdp", n_shard, 1), cot_across, exchange(cot_across, "fsdp", n_shard, 1)]
    down_beside = exchange(down_own, "fsdp", n_shard, 1)
    half_act, half_dn, one_lo, one_hi, dcot, gu_full, own_mid = call(
        functools.partial(mlp_kernel, n_shard, n_rep, True),
        [idx, normed_mid, mid, down_own, down_beside] + cot + gu,
        (
            shape((row_count, model), F32),
            shape((group_rows, model), F32),
            shape((middle, 2 * slab_rows, chunk), BF16),
            shape((middle, 2 * slab_rows, chunk), BF16),
            shape((group_rows, model), BF16),
            shape((model, 2 * ff), BF16),
            shape((group_rows, width), BF16),
        ),
        [
            pltpu.VMEM((n_rep, 2 * slab_rows, chunk), BF16),
            pltpu.VMEM((2 * chunk, model), BF16),
            pltpu.VMEM((group_rows, 2 * chunk), BF16),
            pltpu.SemaphoreType.DMA((6,)),
            pltpu.SemaphoreType.DMA((2,)),
            pltpu.SemaphoreType.DMA((n_shard,)),
        ],
        micros=MICROS[1],
        raw=range(3, 5 + 2 * n_shard + 2),
    )
    down_across, _ = lax.optimization_barrier((down_across, half_act))
    down_corner = exchange(down_across, "fsdp", n_shard, 1)
    out_act, d_normed_mid, two_lo, two_hi = call(
        functools.partial(mlp_kernel, n_shard, n_rep, False),
        [idx, normed_mid, half_act, live, down_across, down_corner, dcot, gu_full, own_mid, half_dn],
        (
            shape((row_count, model), F32),
            shape((group_rows, model), F32),
            shape((middle, slab_rows, chunk), BF16),
            shape((middle, slab_rows, chunk), BF16),
        ),
        [
            pltpu.VMEM((n_rep, slab_rows, chunk), BF16),
            pltpu.VMEM((2 * chunk, model), BF16),
            pltpu.SemaphoreType.DMA((2,)),
        ],
        micros=MICROS[2],
        raw=(4, 5),
    )
    one = sum_over_replicas(one_lo, one_hi, n_rep)
    two = sum_over_replicas(two_lo, two_hi, n_rep)
    in_grad, a_lo, a_hi = call(
        functools.partial(attn_backward_kernel, n_shard, n_rep),
        [idx, x_all, normed, query, keyval, mixed, mid, cosine, sine, gains, wq_full, wkv_full, wo_full,
         d_normed_mid, dcot],
        (
            shape((row_count, model), F32),
            shape((middle,) + a_slab, BF16),
            shape((middle,) + a_slab, BF16),
        ),
        [
            pltpu.VMEM((group_rows, model), BF16),
            pltpu.VMEM((group_rows, QW), BF16),
            pltpu.VMEM((group_rows, QW), BF16),
            pltpu.VMEM((group_rows, kv_width), BF16),
            pltpu.VMEM((a_rows, model), F32),
        ],
        micros=MICROS[3],
    )
    attn = sum_over_replicas(a_lo, a_hi, n_rep)
    grad_down, grad_gateup = call(
        functools.partial(unpack_mlp_kernel, n_rep, n_shard),
        [idx] + list(one) + list(two),
        (shape((w_down.shape[1], model), F32), shape((width, 2 * ff), F32)),
        micros=3,
    )
    grad_query, grad_keyval, grad_out, gain_rows = call(
        functools.partial(unpack_attn_kernel, n_rep),
        [idx] + list(attn),
        (
            shape((width, model), F32),
            shape((width, kv_width), F32),
            shape((width, model), F32),
            shape((8, model), F32),
        ),
        [pltpu.VMEM((a_rows, model), F32)],
        micros=2,
    )
    own_gains = lax.dynamic_slice(gain_rows, (0, shard * width), (2, width))
    return (
        out_act,
        in_grad,
        grad_query[None],
        grad_keyval[None],
        grad_out[None],
        grad_gateup[None],
        grad_down[None],
        own_gains[:1],
        own_gains[1:],
    )


def solution(mesh):
    placed = (
        P(("rep", "fsdp"), None),
        P(("rep", "fsdp")),
        P(("rep", "fsdp")),
        P(None, "fsdp", None),
        P(None, "fsdp", None),
        P(None, "fsdp", None),
        P(None, "fsdp", None),
        P(None, "fsdp", None),
        P(None, "fsdp"),
        P(None, "fsdp"),
        P(("rep", "fsdp"), None),
    )
    return jax.shard_map(
        functools.partial(on_device, mesh.shape["rep"], mesh.shape["fsdp"]),
        mesh=mesh,
        in_specs=placed,
        out_specs=(
            P(("rep", "fsdp"), None),
            P(("rep", "fsdp"), None),
            P(None, "fsdp", None),
            P(None, "fsdp", None),
            P(None, "fsdp", None),
            P(None, "fsdp", None),
            P(None, "fsdp", None),
            P(None, "fsdp"),
            P(None, "fsdp"),
        ),
        check_vma=False,
    )
```

```python
import functools

import jax
import jax.numpy as jnp
from jax import lax
from jax.experimental import pallas as pl
from jax.experimental.pallas import tpu as pltpu
from jax.sharding import PartitionSpec as P

HEADS = 9
KVH = 3
HD = 64
LEN = 64
norm_eps = 1e-05
rope_base = 100000.0

BLOCK = 128
PAIRS = 5
QW = PAIRS * 128
GROUP = 4
PREPARE_VMEM = 60
MICROS = (7, 6, 6, 3, 4, 4)
F32 = jnp.float32
BF16 = jnp.bfloat16


def mm(left, right):
    return jnp.dot(left, right, preferred_element_type=F32)


def mm_nt(left, right):
    return lax.dot_general(left, right, (((1,), (1,)), ((), ())), preferred_element_type=F32)


def mm_tn(left, right):
    return lax.dot_general(left, right, (((0,), (0,)), ((), ())), preferred_element_type=F32)


def inverse_rms(stream):
    return lax.rsqrt(jnp.mean(stream * stream, axis=-1, keepdims=True) + norm_eps)


def lane_index(shape):
    return lax.broadcasted_iota(jnp.int32, shape, 1)


def own_columns(shard, rows, width):
    row = lax.broadcasted_iota(jnp.int32, (rows, width), 0)
    column = lax.broadcasted_iota(jnp.int32, (rows, width), 1)
    return (row == column + shard * width).astype(BF16)


def swapped(values, first_half):
    return jnp.where(first_half, pltpu.roll(values, 96, 1), pltpu.roll(values, 32, 1))


def split_heads(keyval):
    low = lane_index((BLOCK, 128)) < HD
    slices = [keyval[:, 128 * part : 128 * part + 128].astype(F32) for part in range(3)]

    def pair(piece, is_low):
        kept = jnp.where(low, piece, 0.0) if is_low else jnp.where(low, 0.0, piece)
        moved = pltpu.roll(kept, HD, 1)
        kept, moved = kept.astype(BF16), moved.astype(BF16)
        return (kept, moved) if is_low else (moved, kept)

    keys = [pair(slices[0], True), pair(slices[0], False), pair(slices[1], True)]
    values = [pair(slices[1], False), pair(slices[2], True), pair(slices[2], False)]
    return keys, values


def pair_operand(parts, pair):
    first = parts[(2 * pair) * KVH // HEADS][0]
    if 2 * pair + 1 >= HEADS:
        return first
    return jnp.concatenate([first, parts[(2 * pair + 1) * KVH // HEADS][1]], axis=0)


def attention_mask():
    query = lax.broadcasted_iota(jnp.int32, (BLOCK, BLOCK), 0)
    key = lax.broadcasted_iota(jnp.int32, (BLOCK, BLOCK), 1)
    return (query // LEN == key // LEN) & (query >= key)


def soft_rows(scores, allowed):
    halves = []
    for start in range(0, scores.shape[1], BLOCK):
        part = jnp.where(allowed, scores[:, start : start + BLOCK], -1e30)
        part = jnp.exp(part - jnp.max(part, axis=-1, keepdims=True))
        halves.append(part * (1.0 / jnp.sum(part, axis=-1, keepdims=True)))
    return halves


def joined(halves):
    return halves[0] if len(halves) == 1 else jnp.concatenate(halves, axis=1)


def prepare_kernel(idx, wq, wkv, wo, wgu, tokens, grad, positions, gain_attn, gain_mlp,
                   own_ref, send_ref, gu_ref, cot_ref, kv_all, tok_all, grad_all, codes, sem):
    width, kv_width = wkv.shape
    model = own_ref.shape[1]
    side = idx[1] & 1
    ff = gu_ref.shape[1]
    across = pl.ds(pl.multiple_of(side * ff, 128), ff)
    waits = [
        pltpu.make_async_copy(wkv, kv_all, sem.at[0]),
        pltpu.make_async_copy(wq, own_ref.at[pl.ds(0, width)], sem.at[1]),
        pltpu.make_async_copy(wo, own_ref.at[pl.ds(width, width)], sem.at[2]),
        pltpu.make_async_copy(tokens, tok_all, sem.at[3]),
        pltpu.make_async_copy(grad, grad_all, sem.at[4]),
        pltpu.make_async_copy(wgu.at[:, across], gu_ref, sem.at[5]),
    ]
    for wait in waits:
        wait.start()
    count = send_ref.shape[0] - BLOCK - 16
    codes[...] = jnp.zeros_like(codes)
    codes[0:1, :BLOCK] = (positions[...] >> 6).astype(F32)
    codes[1:2, :BLOCK] = (positions[...] & 63).astype(F32)
    codes[2:3, :width] = gain_attn[...].astype(F32)
    codes[3:4, :width] = gain_mlp[...].astype(F32)
    small = codes[...].astype(BF16)
    own_ref[2 * count + BLOCK :, :] = small
    send_ref[count + BLOCK :, :] = small
    rest = model - kv_width
    top = width - width * rest // model
    waits[0].wait()
    own_ref[2 * width : 2 * count, :kv_width] = kv_all[:top, :]
    own_ref[2 * width : 3 * width - top, kv_width:] = kv_all[top:, :rest]
    own_ref[3 * width - top : 2 * count, kv_width:] = kv_all[top:, rest:]
    waits[3].wait()
    rows = tok_all[...].T
    own_ref[2 * count : 2 * count + BLOCK, :] = rows
    send_ref[count : count + BLOCK, :] = rows
    waits[1].wait()
    waits[2].wait()
    send_ref[:count, :] = own_ref[pl.ds(pl.multiple_of(side * count, 16), count), :]
    waits[4].wait()
    cot_ref[...] = (grad_all[...].T.astype(F32) * live_rows(idx)).astype(BF16)
    waits[5].wait()


def live_rows(idx):
    slot = lax.broadcasted_iota(jnp.int32, (BLOCK, 1), 0) // LEN
    return (slot < idx[2]).astype(F32)


def attn_forward_kernel(n_shard, idx, *refs):
    packs = refs[:6]
    (x_ref, nrm_ref, q_ref, kv_ref, mix_ref, mid_ref, nmid_ref, cos_ref, sin_ref, gain_ref,
     wq_full, wkv_full, wo_full, query_all, keyval_all, pack_all, small, sem, tok_sem, small_sem) = refs[6:]
    shard = idx[0]
    side = idx[1] & 1
    model = x_ref.shape[1]
    width = model // n_shard
    count = pack_all.shape[1] // 2
    waits = []
    pieces = [(0, packs[0], None), (1, packs[1], None), (2, packs[2], side), (2, packs[3], 1 - side),
              (3, packs[4], side), (3, packs[5], 1 - side)]
    for number, (part, source, which) in enumerate(pieces):
        target = pack_all.at[part]
        size = 2 * count
        if which is not None:
            target = pack_all.at[part, pl.ds(pl.multiple_of(which * count, 16), count)]
            size = count
        waits.append(pltpu.make_async_copy(source.at[pl.ds(0, size)], target, sem.at[number]))
        if number not in (3, 5):
            tokens_to = x_ref.at[pl.ds(part * BLOCK, BLOCK)]
            waits.append(pltpu.make_async_copy(source.at[pl.ds(size, BLOCK)], tokens_to, tok_sem.at[part]))
            rest = source.at[pl.ds(size + BLOCK, 16)]
            waits.append(pltpu.make_async_copy(rest, small.at[part], small_sem.at[part]))
    for wait in waits:
        wait.start()
    wq_full[:, model:] = jnp.zeros((model, QW - model), BF16)
    wo_full[model:, :] = jnp.zeros((QW - model, model), BF16)
    for wait in waits:
        wait.wait()
    gains = jnp.zeros((16, model), F32)
    kv_width = wkv_full.shape[1]
    rest = model - kv_width
    top = width - width * rest // model
    for part in range(n_shard):
        at = pl.multiple_of((shard ^ part) * width, 16)
        wq_full[pl.ds(at, width), :model] = pack_all[part, :width, :]
        wo_full[pl.ds(at, width), :] = pack_all[part, width : 2 * width, :]
        wkv_full[pl.ds(at, top), :] = pack_all[part, 2 * width :, :kv_width]
        low = pl.ds(pl.multiple_of(at + top, 16), width - top)
        wkv_full[low, :rest] = pack_all[part, 2 * width : 3 * width - top, model - rest :]
        wkv_full[low, rest:] = pack_all[part, 3 * width - top :, model - rest :]
        row = lax.broadcasted_iota(jnp.int32, (256, model), 0)
        column = lax.broadcasted_iota(jnp.int32, (256, model), 1)
        place = ((column == row + at) & (row < width)).astype(BF16)
        gains = gains + mm(small[part, :, :256], place)
    gain_ref[...] = gains
    half = HD // 2
    step = lax.broadcasted_iota(jnp.int32, (half, 1), 0).astype(F32)
    frequency = jnp.exp(step * (-2.0 / HD * jnp.log(F32(rope_base))))
    for part in range(n_shard):
        codes = small[part].astype(F32)
        position = codes[0:1, :BLOCK] * 64.0 + codes[1:2, :BLOCK]
        angle = frequency * position
        rows = pl.ds(part * BLOCK, BLOCK)
        cos_ref[rows, :] = jnp.concatenate([jnp.cos(angle)] * 4, axis=0).T
        sin_ref[rows, :] = jnp.concatenate([jnp.sin(angle)] * 4, axis=0).T
    allowed = attention_mask()
    lane = lane_index((BLOCK, 128))
    first_half = lane % HD < half
    gain_attn = gains[2:3, :]
    gain_mlp = gains[3:4, :]

    for part in range(n_shard):
        rows = pl.ds(part * BLOCK, BLOCK)
        stream = x_ref[rows, :].astype(F32)
        nrm_ref[rows, :] = (stream * inverse_rms(stream) * gain_attn).astype(BF16)
    query_all[...] = mm(nrm_ref[...], wq_full[...])
    keyval_all[...] = mm(nrm_ref[...], wkv_full[...])

    heads = []
    for number in range(n_shard):
        rows = pl.ds(number * BLOCK, BLOCK)
        cosine = cos_ref[rows, :]
        sine = sin_ref[rows, :]
        sine = jnp.where(first_half, -sine, sine)

        def rope(values):
            return values * cosine + swapped(values, first_half) * sine

        kv_ref[rows, :128] = rope(keyval_all[rows, :128]).astype(BF16)
        second = keyval_all[rows, 128:256]
        kv_ref[rows, 128:256] = jnp.where(lane < HD, rope(second), second).astype(BF16)
        kv_ref[rows, 256:] = keyval_all[rows, 256:].astype(BF16)
        for pair in range(PAIRS):
            columns = slice(128 * pair, 128 * pair + 128)
            q_ref[rows, columns] = (rope(query_all[rows, columns]) * HD ** (-0.5)).astype(BF16)
        heads.append(split_heads(kv_ref[rows, :]))
    for start in range(0, n_shard, GROUP):
        units = [(number, pair) for number in range(start, start + GROUP) for pair in range(PAIRS)]
        scores, probs = {}, {}
        for number, pair in units:
            query = q_ref[number * BLOCK : (number + 1) * BLOCK, 128 * pair : 128 * pair + 128]
            scores[number, pair] = mm_nt(query, pair_operand(heads[number][0], pair))
        for unit in units:
            probs[unit] = joined(soft_rows(scores[unit], allowed)).astype(BF16)
        for number, pair in units:
            mixed = mm(probs[number, pair], pair_operand(heads[number][1], pair))
            mix_ref[number * BLOCK : (number + 1) * BLOCK, 128 * pair : 128 * pair + 128] = mixed.astype(BF16)
    stream_mid = x_ref[...].astype(F32) + mm(mix_ref[...], wo_full[...])
    mid_ref[...] = stream_mid
    nmid_ref[...] = (stream_mid * inverse_rms(stream_mid) * gain_mlp).astype(BF16)


def bit_reverse(value, total):
    result = jnp.zeros_like(value)
    bit = 1
    while bit < total:
        result = result * 2 + (value & 1)
        value = value >> 1
        bit *= 2
    return result


def spread(target, member, n_rep, first_row, slab, value):
    to = bit_reverse(member ^ slab, n_rep)
    target[to, first_row : first_row + value.shape[0], :] = value.astype(BF16)


def mlp_kernel(n_shard, n_rep, first_call, idx, *refs):
    if first_call:
        (nmid_ref, mid_ref, wd_own, wd_other), cot, wgu = refs[:4], refs[4 : 4 + n_shard], refs[4 + n_shard : -13]
        (act_ref, dn_ref, lo_ref, hi_ref, dcot_ref, w_full, own_ref, all_ref, wd_pair, wide_ref, sem, wd_sem,
         cot_sem) = refs[-13:]
    else:
        (nmid_ref, act_in, wd_own, wd_other, dcot_ref, w_full, own_ref, dn_in, act_ref, dn_ref, lo_ref,
         hi_ref, all_ref, wd_pair, wd_sem) = refs
    shard = idx[0]
    member = idx[1]
    first = 0 if first_call else 2
    model = nmid_ref.shape[1]
    ff = w_full.shape[1] // 2
    chunk = ff // n_shard
    waits = []
    for part, source in ((first, wd_own), (first + 1, wd_other)):
        at = pl.multiple_of(((shard ^ part) & 1) * chunk, 128)
        waits.append(pltpu.make_async_copy(source, wd_pair.at[:, pl.ds(at, chunk)], wd_sem.at[part - first]))
    if first_call:
        width = model // n_shard
        side = member & 1
        pieces = [(0, wgu[0], None), (1, wgu[1], None), (2, wgu[2], side), (2, wgu[3], 1 - side),
                  (3, wgu[4], side), (3, wgu[5], 1 - side)]
        for number, (part, source, which) in enumerate(pieces):
            down = pl.ds(pl.multiple_of((shard ^ part) * width, 16), width)
            if which is None:
                target = w_full.at[down]
            else:
                target = w_full.at[down, pl.ds(pl.multiple_of(which * ff, 128), ff)]
            waits.append(pltpu.make_async_copy(source, target, sem.at[number]))
        for part in range(n_shard):
            waits.append(
                pltpu.make_async_copy(cot[part], dcot_ref.at[pl.ds(part * BLOCK, BLOCK)], cot_sem.at[part])
            )
    for wait in waits:
        wait.start()
    if first_call:
        own_ref[...] = mm(nmid_ref[...], own_columns(shard, model, width)).astype(BF16)
    for wait in waits:
        wait.wait()
    normed_mid = nmid_ref[...]
    d_branch = dcot_ref[...]
    base = ((shard ^ first) >> 1) * 2 * chunk
    gate_at = pl.ds(pl.multiple_of(base, 256), 2 * chunk)
    up_at = pl.ds(pl.multiple_of(base + ff, 256), 2 * chunk)
    gate = mm(normed_mid, w_full[:, gate_at])
    up = mm(normed_mid, w_full[:, up_at])
    d_hidden = mm(d_branch, wd_pair[...])
    sigmoid = 0.5 * jnp.tanh(0.5 * gate) + 0.5
    silu = gate * sigmoid
    hidden = (silu * up).astype(BF16)
    d_gate = (d_hidden * up * sigmoid * (1.0 + gate * (1.0 - sigmoid))).astype(BF16)
    d_up = (d_hidden * silu).astype(BF16)
    rows = all_ref.shape[1]
    if first_call:
        wide_ref[...] = hidden
        own_hidden = wide_ref[:, pl.ds(pl.multiple_of((shard & 1) * chunk, 128), chunk)]
        rows = rows // 2
        grad_down = mm_tn(d_branch, own_hidden)
        for slab in range(n_rep):
            spread(all_ref, member, n_rep, rows, slab, grad_down[slab * rows : (slab + 1) * rows])
    slab = 0
    for piece in (d_gate, d_up):
        grad = mm_tn(own_ref[...], piece)
        for column in range(0, 2 * chunk, chunk):
            for row in range(0, grad.shape[0], rows):
                spread(all_ref, member, n_rep, 0, slab, grad[row : row + rows, column : column + chunk])
                slab += 1
    middle = n_rep // 2
    lo_ref[...] = all_ref[:middle]
    hi_ref[...] = all_ref[middle:]
    d_normed = mm_nt(d_gate, w_full[:, gate_at]) + mm_nt(d_up, w_full[:, up_at])
    added = mm_nt(hidden[:BLOCK], wd_pair[...])
    if first_call:
        dn_ref[...] = d_normed
        act_ref[...] = mid_ref[:BLOCK, :] + added
    else:
        dn_ref[...] = dn_in[...] + d_normed
        act_ref[...] = ((act_in[...] + added) * live_rows(idx)).T


def residual_backward_kernel(n_shard, idx, mid_ref, dn_ref, dcot_ref, mix_ref, gain_ref, wo_full,
                             dattn_ref, dmix_ref, dmid_ref, gout_ref, gain_out):
    model = mid_ref.shape[1]
    stream_mid = mid_ref[...]
    inv_mlp = inverse_rms(stream_mid)
    d_normed_mid = dn_ref[...]
    sum_mlp = jnp.sum(d_normed_mid * stream_mid * inv_mlp, axis=0, keepdims=True)
    scaled = d_normed_mid * gain_ref[3:4, :]
    d_mid = (
        dcot_ref[...].astype(F32)
        + inv_mlp * scaled
        - inv_mlp**3 * stream_mid * jnp.mean(scaled * stream_mid, axis=-1, keepdims=True)
    )
    dmid_ref[...] = d_mid[:BLOCK, :]
    dattn_ref[...] = d_mid.astype(BF16)
    dmix_ref[...] = mm_nt(dattn_ref[...], wo_full[...]).astype(BF16)
    own_mixed = mm(mix_ref[:, :model], own_columns(idx[0], model, gout_ref.shape[0])).astype(BF16)
    gout_ref[...] = mm_tn(own_mixed, dattn_ref[...])
    gain_out[...] = jnp.broadcast_to(sum_mlp, gain_out.shape)


def heads_backward_kernel(first_row, idx, q_ref, kv_ref, dmix_ref, cos_ref, sin_ref, dq_ref, dkv_ref):
    half = HD // 2
    allowed = attention_mask()
    lane = lane_index((BLOCK, 128))
    first_half = lane % HD < half
    low = lane < HD
    blocks = range(dq_ref.shape[0] // BLOCK)
    units = [(number, pair) for number in blocks for pair in range(PAIRS)]
    rows = [pl.ds(first_row + number * BLOCK, BLOCK) for number in blocks]
    columns = [slice(128 * pair, 128 * pair + 128) for pair in range(PAIRS)]
    heads = [split_heads(kv_ref[rows[number], :]) for number in blocks]
    scores, d_probs = {}, {}
    for number, pair in units:
        keys, values = heads[number]
        scores[number, pair] = mm_nt(q_ref[rows[number], columns[pair]], pair_operand(keys, pair))
        d_probs[number, pair] = mm_nt(dmix_ref[rows[number], columns[pair]], pair_operand(values, pair))
    probs, d_scores = {}, {}
    for unit in units:
        soft = soft_rows(scores[unit], allowed)
        probs[unit] = joined(soft).astype(BF16)
        d_soft = []
        for side, part in enumerate(soft):
            d_part = d_probs[unit][:, side * BLOCK : (side + 1) * BLOCK]
            d_soft.append(part * (d_part - jnp.sum(d_part * part, axis=-1, keepdims=True)))
        d_scores[unit] = joined(d_soft).astype(BF16)
    d_query, d_key_pair, d_value_pair = {}, {}, {}
    for number, pair in units:
        keys, _ = heads[number]
        d_query[number, pair] = mm(d_scores[number, pair], pair_operand(keys, pair))
        d_key_pair[number, pair] = mm_tn(d_scores[number, pair], q_ref[rows[number], columns[pair]])
        d_value_pair[number, pair] = mm_tn(probs[number, pair], dmix_ref[rows[number], columns[pair]])

    def collected(pieces, number, head, to_low):
        sides = [None, None]
        for query_head in range(HEADS):
            if query_head * KVH // HEADS == head:
                pair, side = divmod(query_head, 2)
                piece = pieces[number, pair][side * BLOCK : (side + 1) * BLOCK]
                sides[side] = piece if sides[side] is None else sides[side] + piece
        keep, move = (sides[0], sides[1]) if to_low else (sides[1], sides[0])
        total = keep if move is None else keep + pltpu.roll(move, HD, 1)
        return total

    for number in blocks:
        cosine = cos_ref[rows[number], :]
        sine = sin_ref[rows[number], :]
        sine = jnp.where(first_half, sine, -sine)

        def rope_back(grad):
            return grad * cosine + swapped(grad, first_half) * sine

        to = pl.ds(number * BLOCK, BLOCK)
        for pair in range(PAIRS):
            dq_ref[to, columns[pair]] = rope_back(d_query[number, pair] * HD ** (-0.5)).astype(BF16)
        key = [collected(d_key_pair, number, head, head % 2 == 0) for head in range(KVH)]
        value = [collected(d_value_pair, number, head, head % 2 == 1) for head in range(KVH)]
        dkv_ref[to, :128] = rope_back(jnp.where(low, key[0], key[1])).astype(BF16)
        dkv_ref[to, 128:256] = jnp.where(low, rope_back(key[2]), value[0]).astype(BF16)
        dkv_ref[to, 256:] = jnp.where(low, value[1], value[2]).astype(BF16)


def input_backward_kernel(n_shard, n_rep, idx, x_ref, nrm_ref, gain_ref, wq_full, wkv_full, dmid_ref, gout_ref,
                          gain_mlp_ref, dq_one, dq_two, dkv_one, dkv_two, din_ref, a_lo, a_hi, a_all, dq_all, dkv_all):
    model = x_ref.shape[1]
    width = gout_ref.shape[0]
    half_rows = dq_one.shape[0]
    dq_all[:half_rows, :] = dq_one[...]
    dq_all[half_rows:, :] = dq_two[...]
    dkv_all[:half_rows, :] = dkv_one[...]
    dkv_all[half_rows:, :] = dkv_two[...]
    own_normed = mm(nrm_ref[...], own_columns(idx[0], model, width)).astype(BF16)
    kv_width = dkv_all.shape[1]
    a_all[:width, :] = mm_tn(own_normed, dq_all[:, :model])
    a_all[width : 2 * width, :] = gout_ref[...]
    a_all[2 * width : 3 * width, :kv_width] = mm_tn(own_normed, dkv_all[...])
    a_all[2 * width : 3 * width, kv_width:] = jnp.zeros((width, model - kv_width), F32)
    d_normed = mm_nt(dq_all[...], wq_full[...]) + mm_nt(dkv_all[...], wkv_full[...])
    stream = x_ref[...].astype(F32)
    inv_attn = inverse_rms(stream)
    sum_attn = jnp.sum(d_normed * stream * inv_attn, axis=0, keepdims=True)
    tail = a_all.shape[0] - 3 * width
    row = lax.broadcasted_iota(jnp.int32, (tail, model), 0)
    a_all[3 * width :, :] = jnp.where(row == 0, sum_attn, jnp.where(row == 1, gain_mlp_ref[:1, :], 0.0))
    rows = a_all.shape[0] // n_rep
    middle = n_rep // 2
    for slab in range(n_rep):
        to = bit_reverse(idx[1] ^ slab, n_rep)
        piece = a_all[slab * rows : (slab + 1) * rows, :].astype(BF16)

        @pl.when(to < middle)
        def _():
            a_lo[to] = piece

        @pl.when(to >= middle)
        def _():
            a_hi[to - middle] = piece

    own_in = d_normed[:BLOCK, :] * gain_ref[2:3, :]
    own_stream = stream[:BLOCK, :]
    own_inv = inv_attn[:BLOCK, :]
    din_ref[...] = (
        dmid_ref[...]
        + own_inv * own_in
        - own_inv**3 * own_stream * jnp.mean(own_in * own_stream, axis=-1, keepdims=True)
    ).T


def fetch(first, second, member, slab, n_rep, target, rows):
    at = bit_reverse(member ^ slab, n_rep)
    middle = n_rep // 2

    @pl.when(at < middle)
    def _():
        target[pl.ds(slab * rows, rows), :] = first[at].astype(F32)

    @pl.when(at >= middle)
    def _():
        target[pl.ds(slab * rows, rows), :] = second[at - middle].astype(F32)


def unpack_mlp_kernel(n_rep, n_shard, idx, one_lo, one_hi, two_lo, two_hi, down_ref, gu_ref):
    shard = idx[0]
    member = idx[1]
    middle = n_rep // 2
    rows, chunk = two_lo.shape[1:]
    ff = gu_ref.shape[1] // 2
    groups = gu_ref.shape[0] // rows

    def place_gateup(slab, pair, piece):
        up, rest = divmod(slab, 2 * groups)
        column, group = divmod(rest, groups)
        base = ((shard ^ (2 * pair)) >> 1) * 2 * chunk + column * chunk + up * ff
        gu_ref[group * rows : (group + 1) * rows, pl.ds(pl.multiple_of(base, 128), chunk)] = piece

    for slab in range(n_rep):
        at = bit_reverse(member ^ slab, n_rep)

        def place(one, two, where):
            piece = one[where].astype(F32)
            place_gateup(slab, 0, piece[:rows])
            down_ref[slab * rows : (slab + 1) * rows, :] = piece[rows:]
            place_gateup(slab, 1, two[where].astype(F32))

        @pl.when(at < middle)
        def _():
            place(one_lo, two_lo, at)

        @pl.when(at >= middle)
        def _():
            place(one_hi, two_hi, at - middle)


def unpack_attn_kernel(n_rep, idx, first, second, q_ref, kv_ref, o_ref, gain_ref, a_all):
    rows = first.shape[1]
    for slab in range(n_rep):
        fetch(first, second, idx[1], slab, n_rep, a_all, rows)
    width = q_ref.shape[0]
    q_ref[...] = a_all[:width, :]
    o_ref[...] = a_all[width : 2 * width, :]
    kv_ref[...] = a_all[2 * width : 3 * width, : kv_ref.shape[1]]
    gain_ref[...] = a_all[3 * width : 3 * width + 8, :]


def call(body, operands, outs, scratch=(), micros=1, vmem=24, raw=()):
    in_vmem = pl.BlockSpec(memory_space=pltpu.VMEM)
    in_hbm = pl.BlockSpec(memory_space=pltpu.HBM)
    specs = [in_hbm if number in raw else in_vmem for number in range(1, len(operands))]
    return pl.pallas_call(
        body,
        out_shape=outs,
        in_specs=[pl.BlockSpec(memory_space=pltpu.SMEM)] + specs,
        out_specs=jax.tree.map(lambda _: in_vmem, outs),
        scratch_shapes=list(scratch),
        compiler_params=pltpu.CompilerParams(vmem_limit_bytes=vmem * 2**20),
        cost_estimate=pl.CostEstimate(flops=int(micros * 1e9), bytes_accessed=2**20, transcendentals=0),
    )(*operands)


def shape(dims, dtype):
    return jax.ShapeDtypeStruct(dims, dtype)


def exchange(value, axis, total, mask):
    return lax.ppermute(value, axis, [(member, member ^ mask) for member in range(total)])


def replica_steps(low, high, total):
    mask = 1
    while True:
        arrived = exchange(high, "rep", total, mask)
        held = (low.astype(F32) + arrived.astype(F32)).astype(BF16)
        yield held
        mask *= 2
        if mask == total:
            break
        low, high = held[: held.shape[0] // 2], held[held.shape[0] // 2 :]
    mask = total // 2
    while True:
        arrived = exchange(held, "rep", total, mask)
        mask //= 2
        if mask == 0:
            yield held, arrived
            return
        held = jnp.concatenate([held, arrived], axis=0)
        yield held


def last_of(steps):
    for result in steps:
        pass
    return result


def after(value, *earlier):
    return lax.optimization_barrier((value,) + earlier)[0]


def on_device(n_rep, n_shard, tokens, positions, seq_count, w_query, w_keyval, w_out, w_gateup, w_down, gain_attn,
              gain_mlp, out_grad):
    row_count, model = tokens.shape
    width = w_query.shape[1]
    ff = w_gateup.shape[2] // 2
    kv_width = w_keyval.shape[2]
    group_rows = n_shard * row_count
    shard = lax.axis_index("fsdp").astype(jnp.int32)
    member = lax.axis_index("rep").astype(jnp.int32)
    idx = jnp.stack([shard, member, seq_count[0]])
    pack_rows = 2 * width + width * kv_width // model
    own_full, half_full, gu_half, cotangent = call(
        prepare_kernel,
        [idx, w_query[0], w_keyval[0], w_out[0], w_gateup[0], tokens.T, out_grad.T, positions[None], gain_attn,
         gain_mlp],
        (
            shape((pack_rows + row_count + 16, model), BF16),
            shape((pack_rows // 2 + row_count + 16, model), BF16),
            shape((width, ff), BF16),
            shape((row_count, model), BF16),
        ),
        [
            pltpu.VMEM((width, kv_width), BF16),
            pltpu.VMEM((model, row_count), BF16),
            pltpu.VMEM((model, row_count), BF16),
            pltpu.VMEM((16, model), F32),
            pltpu.SemaphoreType.DMA((6,)),
        ],
        micros=1,
        vmem=PREPARE_VMEM,
        raw=range(1, 7),
    )
    direct = exchange(half_full, "fsdp", n_shard, 2)
    around = exchange(direct[: pack_rows // 2], "rep", n_rep, 1)
    packs = [own_full, exchange(own_full, "fsdp", n_shard, 1), direct, around,
             exchange(direct, "fsdp", n_shard, 1), exchange(around, "fsdp", n_shard, 1)]
    gu_direct = exchange(gu_half, "fsdp", n_shard, 2)
    idx_late, gu_direct = lax.optimization_barrier((idx, gu_direct))
    gu_around = exchange(gu_direct, "rep", n_rep, 1)
    cot_across = exchange(cotangent, "fsdp", n_shard, 2)
    down_across = exchange(w_down[0].T, "fsdp", n_shard, 2)
    (x_all, normed, query, keyval, mixed, mid, normed_mid, cosine, sine, gains, wq_full, wkv_full, wo_full) = call(
        functools.partial(attn_forward_kernel, n_shard),
        [idx_late] + packs,
        (
            shape((group_rows, model), BF16),
            shape((group_rows, model), BF16),
            shape((group_rows, QW), BF16),
            shape((group_rows, kv_width), BF16),
            shape((group_rows, QW), BF16),
            shape((group_rows, model), F32),
            shape((group_rows, model), BF16),
            shape((group_rows, 128), F32),
            shape((group_rows, 128), F32),
            shape((16, model), F32),
            shape((model, QW), BF16),
            shape((model, kv_width), BF16),
            shape((QW, model), BF16),
        ),
        [
            pltpu.VMEM((group_rows, QW), F32),
            pltpu.VMEM((group_rows, kv_width), F32),
            pltpu.VMEM((n_shard, pack_rows, model), BF16),
            pltpu.VMEM((n_shard, 16, model), BF16),
            pltpu.SemaphoreType.DMA((6,)),
            pltpu.SemaphoreType.DMA((n_shard,)),
            pltpu.SemaphoreType.DMA((n_shard,)),
        ],
        micros=MICROS[0],
        raw=range(1, 7),
    )
    middle = n_rep // 2
    chunk = ff // n_shard
    slab_rows = width * 4 // n_rep
    a_rows = 3 * width + 16
    a_slab = (a_rows // n_rep, model)
    gu_own, cot_own, down_own, gu_direct, gu_around, cot_across, down_across, _ = lax.optimization_barrier(
        (w_gateup[0], cotangent, w_down[0].T, gu_direct, gu_around, cot_across, down_across, gains)
    )
    gu = [gu_own, exchange(gu_own, "fsdp", n_shard, 1), gu_direct, gu_around,
          exchange(gu_direct, "fsdp", n_shard, 1), exchange(gu_around, "fsdp", n_shard, 1)]
    cot = [cot_own, exchange(cot_own, "fsdp", n_shard, 1), cot_across, exchange(cot_across, "fsdp", n_shard, 1)]
    down_beside = exchange(down_own, "fsdp", n_shard, 1)
    half_act, half_dn, one_lo, one_hi, dcot, gu_full, own_mid = call(
        functools.partial(mlp_kernel, n_shard, n_rep, True),
        [idx, normed_mid, mid, down_own, down_beside] + cot + gu,
        (
            shape((row_count, model), F32),
            shape((group_rows, model), F32),
            shape((middle, 2 * slab_rows, chunk), BF16),
            shape((middle, 2 * slab_rows, chunk), BF16),
            shape((group_rows, model), BF16),
            shape((model, 2 * ff), BF16),
            shape((group_rows, width), BF16),
        ),
        [
            pltpu.VMEM((n_rep, 2 * slab_rows, chunk), BF16),
            pltpu.VMEM((model, 2 * chunk), BF16),
            pltpu.VMEM((group_rows, 2 * chunk), BF16),
            pltpu.SemaphoreType.DMA((6,)),
            pltpu.SemaphoreType.DMA((2,)),
            pltpu.SemaphoreType.DMA((n_shard,)),
        ],
        micros=MICROS[1],
        raw=range(3, 5 + 2 * n_shard + 2),
    )
    down_across, _ = lax.optimization_barrier((down_across, half_act))
    down_corner = exchange(down_across, "fsdp", n_shard, 1)
    out_act, d_normed_mid, two_lo, two_hi = call(
        functools.partial(mlp_kernel, n_shard, n_rep, False),
        [idx, normed_mid, half_act, down_across, down_corner, dcot, gu_full, own_mid, half_dn],
        (
            shape((model, row_count), F32),
            shape((group_rows, model), F32),
            shape((middle, slab_rows, chunk), BF16),
            shape((middle, slab_rows, chunk), BF16),
        ),
        [
            pltpu.VMEM((n_rep, slab_rows, chunk), BF16),
            pltpu.VMEM((model, 2 * chunk), BF16),
            pltpu.SemaphoreType.DMA((2,)),
        ],
        micros=MICROS[2],
        raw=(3, 4),
    )
    one = replica_steps(one_lo, one_hi, n_rep)
    two = replica_steps(two_lo, two_hi, n_rep)
    d_attn, d_mixed, d_mid, part_out, part_gain = call(
        functools.partial(residual_backward_kernel, n_shard),
        [idx, mid, d_normed_mid, dcot, mixed, gains, wo_full],
        (
            shape((group_rows, model), BF16),
            shape((group_rows, QW), BF16),
            shape((row_count, model), F32),
            shape((width, model), F32),
            shape((8, model), F32),
        ),
        micros=MICROS[3],
    )
    halves = []
    for first_row in (0, group_rows // 2):
        d_mixed = after(d_mixed, *([next(one)] if first_row == 0 else [next(one), next(two), halves[0][0]]))
        halves.append(
            call(
                functools.partial(heads_backward_kernel, first_row),
                [idx, query, keyval, d_mixed, cosine, sine],
                (shape((group_rows // 2, QW), BF16), shape((group_rows // 2, kv_width), BF16)),
                micros=MICROS[4],
            )
        )
    d_mid = after(d_mid, next(one), next(two))
    in_grad, a_lo, a_hi = call(
        functools.partial(input_backward_kernel, n_shard, n_rep),
        [idx, x_all, normed, gains, wq_full, wkv_full, d_mid, part_out, part_gain,
         halves[0][0], halves[1][0], halves[0][1], halves[1][1]],
        (
            shape((model, row_count), F32),
            shape((middle,) + a_slab, BF16),
            shape((middle,) + a_slab, BF16),
        ),
        [
            pltpu.VMEM((a_rows, model), F32),
            pltpu.VMEM((group_rows, QW), BF16),
            pltpu.VMEM((group_rows, kv_width), BF16),
        ],
        micros=MICROS[5],
    )
    one, two = last_of(one), last_of(two)
    attn = last_of(replica_steps(a_lo, a_hi, n_rep))
    grad_down, grad_gateup = call(
        functools.partial(unpack_mlp_kernel, n_rep, n_shard),
        [idx] + list(one) + list(two),
        (shape((model, chunk), F32), shape((width, 2 * ff), F32)),
        micros=3,
    )
    grad_query, grad_keyval, grad_out, gain_rows = call(
        functools.partial(unpack_attn_kernel, n_rep),
        [idx] + list(attn),
        (
            shape((width, model), F32),
            shape((width, kv_width), F32),
            shape((width, model), F32),
            shape((8, model), F32),
        ),
        [pltpu.VMEM((a_rows, model), F32)],
        micros=2,
    )
    own_gains = lax.dynamic_slice(gain_rows, (0, shard * width), (2, width))
    return (
        out_act.T,
        in_grad.T,
        grad_query[None],
        grad_keyval[None],
        grad_out[None],
        grad_gateup[None],
        grad_down.T[None],
        own_gains[:1],
        own_gains[1:],
    )


def solution(mesh):
    placed = (
        P(("rep", "fsdp"), None),
        P(("rep", "fsdp")),
        P(("rep", "fsdp")),
        P(None, "fsdp", None),
        P(None, "fsdp", None),
        P(None, "fsdp", None),
        P(None, "fsdp", None),
        P(None, "fsdp", None),
        P(None, "fsdp"),
        P(None, "fsdp"),
        P(("rep", "fsdp"), None),
    )
    return jax.shard_map(
        functools.partial(on_device, mesh.shape["rep"], mesh.shape["fsdp"]),
        mesh=mesh,
        in_specs=placed,
        out_specs=(
            P(("rep", "fsdp"), None),
            P(("rep", "fsdp"), None),
            P(None, "fsdp", None),
            P(None, "fsdp", None),
            P(None, "fsdp", None),
            P(None, "fsdp", None),
            P(None, "fsdp", None),
            P(None, "fsdp"),
            P(None, "fsdp"),
        ),
        check_vma=False,
    )
```

```python
import functools

import jax
import jax.numpy as jnp
from jax import lax
from jax.experimental import pallas as pl
from jax.experimental.pallas import tpu as pltpu
from jax.sharding import PartitionSpec as P

HEADS = 9
KVH = 3
HD = 64
LEN = 64
norm_eps = 1e-05
rope_base = 100000.0

BLOCK = 128
PAIRS = 5
QW = PAIRS * 128
GROUP = 4
PREPARE_VMEM = 60
TURNED = (0, 0, 0)
TIES = ((1, 0), (1, 1), (2, 1))
MICROS = (1, 6, 6, 3, 4, 4)
F32 = jnp.float32
BF16 = jnp.bfloat16


def mm(left, right):
    return jnp.dot(left, right, preferred_element_type=F32)


def mm_nt(left, right):
    return lax.dot_general(left, right, (((1,), (1,)), ((), ())), preferred_element_type=F32)


def mm_tn(left, right):
    return lax.dot_general(left, right, (((0,), (0,)), ((), ())), preferred_element_type=F32)


def inverse_rms(stream):
    return lax.rsqrt(jnp.mean(stream * stream, axis=-1, keepdims=True) + norm_eps)


def lane_index(shape):
    return lax.broadcasted_iota(jnp.int32, shape, 1)


def own_columns(shard, rows, width):
    row = lax.broadcasted_iota(jnp.int32, (rows, width), 0)
    column = lax.broadcasted_iota(jnp.int32, (rows, width), 1)
    return (row == column + shard * width).astype(BF16)


def swapped(values, first_half):
    return jnp.where(first_half, pltpu.roll(values, 96, 1), pltpu.roll(values, 32, 1))


def split_heads(keyval):
    low = lane_index((BLOCK, 128)) < HD
    slices = [keyval[:, 128 * part : 128 * part + 128].astype(F32) for part in range(3)]

    def pair(piece, is_low):
        kept = jnp.where(low, piece, 0.0) if is_low else jnp.where(low, 0.0, piece)
        moved = pltpu.roll(kept, HD, 1)
        kept, moved = kept.astype(BF16), moved.astype(BF16)
        return (kept, moved) if is_low else (moved, kept)

    keys = [pair(slices[0], True), pair(slices[0], False), pair(slices[1], True)]
    values = [pair(slices[1], False), pair(slices[2], True), pair(slices[2], False)]
    return keys, values


def pair_operand(parts, pair):
    first = parts[(2 * pair) * KVH // HEADS][0]
    if 2 * pair + 1 >= HEADS:
        return first
    return jnp.concatenate([first, parts[(2 * pair + 1) * KVH // HEADS][1]], axis=0)


def attention_mask():
    query = lax.broadcasted_iota(jnp.int32, (BLOCK, BLOCK), 0)
    key = lax.broadcasted_iota(jnp.int32, (BLOCK, BLOCK), 1)
    return (query // LEN == key // LEN) & (query >= key)


def soft_rows(scores, allowed):
    halves = []
    for start in range(0, scores.shape[1], BLOCK):
        part = jnp.where(allowed, scores[:, start : start + BLOCK], -1e30)
        part = jnp.exp(part - jnp.max(part, axis=-1, keepdims=True))
        halves.append(part * (1.0 / jnp.sum(part, axis=-1, keepdims=True)))
    return halves


def joined(halves):
    return halves[0] if len(halves) == 1 else jnp.concatenate(halves, axis=1)


def prepare_kernel(idx, wq, wkv, wo, wgu, tokens, grad, positions, gain_attn, gain_mlp,
                   own_ref, send_ref, gu_one, gu_two, cot_ref, kv_all, tok_all, grad_all, codes, sem):
    width, kv_width = wkv.shape
    model = own_ref.shape[1]
    side = idx[1] & 1
    part = gu_one.shape[1]
    across = [pl.ds(pl.multiple_of((2 * side + number) * part, 128), part) for number in range(2)]
    waits = [
        pltpu.make_async_copy(wkv, kv_all, sem.at[0]),
        pltpu.make_async_copy(wq, own_ref.at[pl.ds(0, width)], sem.at[1]),
        pltpu.make_async_copy(wo, own_ref.at[pl.ds(width, width)], sem.at[2]),
        pltpu.make_async_copy(tokens, tok_all, sem.at[3]),
        pltpu.make_async_copy(grad, grad_all, sem.at[4]),
        pltpu.make_async_copy(wgu.at[:, across[0]], gu_one, sem.at[5]),
        pltpu.make_async_copy(wgu.at[:, across[1]], gu_two, sem.at[6]),
    ]
    for wait in waits:
        wait.start()
    count = send_ref.shape[0] - BLOCK - 16
    codes[...] = jnp.zeros_like(codes)
    codes[0:1, :BLOCK] = (positions[...] >> 6).astype(F32)
    codes[1:2, :BLOCK] = (positions[...] & 63).astype(F32)
    codes[2:3, :width] = gain_attn[...].astype(F32)
    codes[3:4, :width] = gain_mlp[...].astype(F32)
    small = codes[...].astype(BF16)
    own_ref[2 * count + BLOCK :, :] = small
    send_ref[count + BLOCK :, :] = small
    rest = model - kv_width
    top = width - width * rest // model
    waits[0].wait()
    own_ref[2 * width : 2 * count, :kv_width] = kv_all[:top, :]
    own_ref[2 * width : 3 * width - top, kv_width:] = kv_all[top:, :rest]
    own_ref[3 * width - top : 2 * count, kv_width:] = kv_all[top:, rest:]
    waits[3].wait()
    rows = tok_all[...].T
    own_ref[2 * count : 2 * count + BLOCK, :] = rows
    send_ref[count : count + BLOCK, :] = rows
    waits[1].wait()
    waits[2].wait()
    send_ref[:count, :] = own_ref[pl.ds(pl.multiple_of(side * count, 16), count), :]
    waits[4].wait()
    cot_ref[...] = (grad_all[...].T.astype(F32) * live_rows(idx)).astype(BF16)
    waits[5].wait()
    waits[6].wait()


def live_rows(idx):
    slot = lax.broadcasted_iota(jnp.int32, (BLOCK, 1), 0) // LEN
    return (slot < idx[2]).astype(F32)


def attn_forward_kernel(n_shard, idx, *refs):
    packs = refs[:6]
    (x_ref, nrm_ref, q_ref, kv_ref, mix_ref, mid_ref, nmid_ref, cos_ref, sin_ref, gain_ref,
     wq_full, wkv_full, wo_full, query_all, keyval_all, pack_all, small, sem, tok_sem, small_sem) = refs[6:]
    shard = idx[0]
    side = idx[1] & 1
    model = x_ref.shape[1]
    width = model // n_shard
    count = pack_all.shape[1] // 2
    waits = []
    pieces = [(0, packs[0], None), (1, packs[1], None), (2, packs[2], side), (2, packs[3], 1 - side),
              (3, packs[4], side), (3, packs[5], 1 - side)]
    for number, (part, source, which) in enumerate(pieces):
        target = pack_all.at[part]
        size = 2 * count
        if which is not None:
            target = pack_all.at[part, pl.ds(pl.multiple_of(which * count, 16), count)]
            size = count
        waits.append(pltpu.make_async_copy(source.at[pl.ds(0, size)], target, sem.at[number]))
        if number not in (3, 5):
            tokens_to = x_ref.at[pl.ds(part * BLOCK, BLOCK)]
            waits.append(pltpu.make_async_copy(source.at[pl.ds(size, BLOCK)], tokens_to, tok_sem.at[part]))
            rest = source.at[pl.ds(size + BLOCK, 16)]
            waits.append(pltpu.make_async_copy(rest, small.at[part], small_sem.at[part]))
    for wait in waits:
        wait.start()
    wq_full[:, model:] = jnp.zeros((model, QW - model), BF16)
    wo_full[model:, :] = jnp.zeros((QW - model, model), BF16)
    for wait in waits:
        wait.wait()
    gains = jnp.zeros((16, model), F32)
    kv_width = wkv_full.shape[1]
    rest = model - kv_width
    top = width - width * rest // model
    for part in range(n_shard):
        at = pl.multiple_of((shard ^ part) * width, 16)
        wq_full[pl.ds(at, width), :model] = pack_all[part, :width, :]
        wo_full[pl.ds(at, width), :] = pack_all[part, width : 2 * width, :]
        wkv_full[pl.ds(at, top), :] = pack_all[part, 2 * width :, :kv_width]
        low = pl.ds(pl.multiple_of(at + top, 16), width - top)
        wkv_full[low, :rest] = pack_all[part, 2 * width : 3 * width - top, model - rest :]
        wkv_full[low, rest:] = pack_all[part, 3 * width - top :, model - rest :]
        row = lax.broadcasted_iota(jnp.int32, (256, model), 0)
        column = lax.broadcasted_iota(jnp.int32, (256, model), 1)
        place = ((column == row + at) & (row < width)).astype(BF16)
        gains = gains + mm(small[part, :, :256], place)
    gain_ref[...] = gains
    half = HD // 2
    step = lax.broadcasted_iota(jnp.int32, (half, 1), 0).astype(F32)
    frequency = jnp.exp(step * (-2.0 / HD * jnp.log(F32(rope_base))))
    for part in range(n_shard):
        codes = small[part].astype(F32)
        position = codes[0:1, :BLOCK] * 64.0 + codes[1:2, :BLOCK]
        angle = frequency * position
        rows = pl.ds(part * BLOCK, BLOCK)
        cos_ref[rows, :] = jnp.concatenate([jnp.cos(angle)] * 4, axis=0).T
        sin_ref[rows, :] = jnp.concatenate([jnp.sin(angle)] * 4, axis=0).T
    allowed = attention_mask()
    lane = lane_index((BLOCK, 128))
    first_half = lane % HD < half
    gain_attn = gains[2:3, :]
    gain_mlp = gains[3:4, :]

    for part in range(n_shard):
        rows = pl.ds(part * BLOCK, BLOCK)
        stream = x_ref[rows, :].astype(F32)
        nrm_ref[rows, :] = (stream * inverse_rms(stream) * gain_attn).astype(BF16)
    query_all[...] = mm(nrm_ref[...], wq_full[...])
    keyval_all[...] = mm(nrm_ref[...], wkv_full[...])

    heads = []
    for number in range(n_shard):
        rows = pl.ds(number * BLOCK, BLOCK)
        cosine = cos_ref[rows, :]
        sine = sin_ref[rows, :]
        sine = jnp.where(first_half, -sine, sine)

        def rope(values):
            return values * cosine + swapped(values, first_half) * sine

        kv_ref[rows, :128] = rope(keyval_all[rows, :128]).astype(BF16)
        second = keyval_all[rows, 128:256]
        kv_ref[rows, 128:256] = jnp.where(lane < HD, rope(second), second).astype(BF16)
        kv_ref[rows, 256:] = keyval_all[rows, 256:].astype(BF16)
        for pair in range(PAIRS):
            columns = slice(128 * pair, 128 * pair + 128)
            q_ref[rows, columns] = (rope(query_all[rows, columns]) * HD ** (-0.5)).astype(BF16)
        heads.append(split_heads(kv_ref[rows, :]))
    for start in range(0, n_shard, GROUP):
        units = [(number, pair) for number in range(start, start + GROUP) for pair in range(PAIRS)]
        scores, probs = {}, {}
        for number, pair in units:
            query = q_ref[number * BLOCK : (number + 1) * BLOCK, 128 * pair : 128 * pair + 128]
            scores[number, pair] = mm_nt(query, pair_operand(heads[number][0], pair))
        for unit in units:
            probs[unit] = joined(soft_rows(scores[unit], allowed)).astype(BF16)
        for number, pair in units:
            mixed = mm(probs[number, pair], pair_operand(heads[number][1], pair))
            mix_ref[number * BLOCK : (number + 1) * BLOCK, 128 * pair : 128 * pair + 128] = mixed.astype(BF16)
    stream_mid = x_ref[...].astype(F32) + mm(mix_ref[...], wo_full[...])
    mid_ref[...] = stream_mid
    nmid_ref[...] = (stream_mid * inverse_rms(stream_mid) * gain_mlp).astype(BF16)


def masks(total, turned):
    steps = []
    while 2 ** len(steps) < total:
        steps.append(2 ** len(steps))
    return steps[turned:] + steps[:turned]


def slab_place(value, steps):
    result = jnp.zeros_like(value)
    for mask in steps:
        result = result * 2 + ((value & mask) != 0).astype(jnp.int32)
    return result


def spread(target, member, steps, first_row, slab, value):
    to = slab_place(member ^ slab, steps)
    target[to, first_row : first_row + value.shape[0], :] = value.astype(BF16)


def mlp_kernel(n_shard, n_rep, first_call, idx, *refs):
    if first_call:
        (nmid_ref, mid_ref, wd_own, wd_other), cot, wgu = refs[:4], refs[4 : 4 + n_shard], refs[4 + n_shard : -13]
        (act_ref, dn_ref, lo_ref, hi_ref, dcot_ref, w_full, own_ref, all_ref, wd_pair, wide_ref, sem, wd_sem,
         cot_sem) = refs[-13:]
    else:
        (nmid_ref, act_in, wd_own, wd_other, dcot_ref, w_full, own_ref, dn_in, act_ref, dn_ref, lo_ref,
         hi_ref, all_ref, wd_pair, wd_sem) = refs
    shard = idx[0]
    member = idx[1]
    first = 0 if first_call else 2
    steps = masks(n_rep, TURNED[0] if first_call else TURNED[1])
    model = nmid_ref.shape[1]
    ff = w_full.shape[1] // 2
    chunk = ff // n_shard
    waits = []
    for part, source in ((first, wd_own), (first + 1, wd_other)):
        at = pl.multiple_of(((shard ^ part) & 1) * chunk, 128)
        waits.append(pltpu.make_async_copy(source, wd_pair.at[:, pl.ds(at, chunk)], wd_sem.at[part - first]))
    if first_call:
        width = model // n_shard
        side = member & 1
        pieces = [(0, wgu[0], None), (1, wgu[1], None)]
        for number in range(8):
            part, rest = divmod(number, 4)
            which = side if rest < 2 else 1 - side
            pieces.append((2 + part, wgu[2 + number], 2 * which + rest % 2))
        for number, (part, source, which) in enumerate(pieces):
            down = pl.ds(pl.multiple_of((shard ^ part) * width, 16), width)
            if which is None:
                target = w_full.at[down]
            else:
                size = ff // 2
                target = w_full.at[down, pl.ds(pl.multiple_of(which * size, 128), size)]
            waits.append(pltpu.make_async_copy(source, target, sem.at[number]))
        for part in range(n_shard):
            waits.append(
                pltpu.make_async_copy(cot[part], dcot_ref.at[pl.ds(part * BLOCK, BLOCK)], cot_sem.at[part])
            )
    for wait in waits:
        wait.start()
    if first_call:
        own_ref[...] = mm(nmid_ref[...], own_columns(shard, model, width)).astype(BF16)
    for wait in waits:
        wait.wait()
    normed_mid = nmid_ref[...]
    d_branch = dcot_ref[...]
    base = ((shard ^ first) >> 1) * 2 * chunk
    gate_at = pl.ds(pl.multiple_of(base, 256), 2 * chunk)
    up_at = pl.ds(pl.multiple_of(base + ff, 256), 2 * chunk)
    gate = mm(normed_mid, w_full[:, gate_at])
    up = mm(normed_mid, w_full[:, up_at])
    d_hidden = mm(d_branch, wd_pair[...])
    sigmoid = 0.5 * jnp.tanh(0.5 * gate) + 0.5
    silu = gate * sigmoid
    hidden = (silu * up).astype(BF16)
    d_gate = (d_hidden * up * sigmoid * (1.0 + gate * (1.0 - sigmoid))).astype(BF16)
    d_up = (d_hidden * silu).astype(BF16)
    rows = all_ref.shape[1]
    if first_call:
        wide_ref[...] = hidden
        own_hidden = wide_ref[:, pl.ds(pl.multiple_of((shard & 1) * chunk, 128), chunk)]
        rows = rows // 2
        grad_down = mm_tn(d_branch, own_hidden)
        for slab in range(n_rep):
            spread(all_ref, member, steps, rows, slab, grad_down[slab * rows : (slab + 1) * rows])
    slab = 0
    for piece in (d_gate, d_up):
        grad = mm_tn(own_ref[...], piece)
        for column in range(0, 2 * chunk, chunk):
            for row in range(0, grad.shape[0], rows):
                spread(all_ref, member, steps, 0, slab, grad[row : row + rows, column : column + chunk])
                slab += 1
    middle = n_rep // 2
    lo_ref[...] = all_ref[:middle]
    hi_ref[...] = all_ref[middle:]
    d_normed = mm_nt(d_gate, w_full[:, gate_at]) + mm_nt(d_up, w_full[:, up_at])
    added = mm_nt(hidden[:BLOCK], wd_pair[...])
    if first_call:
        dn_ref[...] = d_normed
        act_ref[...] = mid_ref[:BLOCK, :] + added
    else:
        dn_ref[...] = dn_in[...] + d_normed
        act_ref[...] = ((act_in[...] + added) * live_rows(idx)).T


def residual_backward_kernel(n_shard, idx, mid_ref, dn_ref, dcot_ref, mix_ref, gain_ref, wo_full,
                             dattn_ref, dmix_ref, dmid_ref, gout_ref, gain_out):
    model = mid_ref.shape[1]
    stream_mid = mid_ref[...]
    inv_mlp = inverse_rms(stream_mid)
    d_normed_mid = dn_ref[...]
    sum_mlp = jnp.sum(d_normed_mid * stream_mid * inv_mlp, axis=0, keepdims=True)
    scaled = d_normed_mid * gain_ref[3:4, :]
    d_mid = (
        dcot_ref[...].astype(F32)
        + inv_mlp * scaled
        - inv_mlp**3 * stream_mid * jnp.mean(scaled * stream_mid, axis=-1, keepdims=True)
    )
    dmid_ref[...] = d_mid[:BLOCK, :]
    dattn_ref[...] = d_mid.astype(BF16)
    dmix_ref[...] = mm_nt(dattn_ref[...], wo_full[...]).astype(BF16)
    own_mixed = mm(mix_ref[:, :model], own_columns(idx[0], model, gout_ref.shape[0])).astype(BF16)
    gout_ref[...] = mm_tn(own_mixed, dattn_ref[...])
    gain_out[...] = jnp.broadcast_to(sum_mlp, gain_out.shape)


def heads_backward_kernel(first_row, idx, q_ref, kv_ref, dmix_ref, cos_ref, sin_ref, dq_ref, dkv_ref):
    half = HD // 2
    allowed = attention_mask()
    lane = lane_index((BLOCK, 128))
    first_half = lane % HD < half
    low = lane < HD
    blocks = range(dq_ref.shape[0] // BLOCK)
    units = [(number, pair) for number in blocks for pair in range(PAIRS)]
    rows = [pl.ds(first_row + number * BLOCK, BLOCK) for number in blocks]
    columns = [slice(128 * pair, 128 * pair + 128) for pair in range(PAIRS)]
    heads = [split_heads(kv_ref[rows[number], :]) for number in blocks]
    scores, d_probs = {}, {}
    for number, pair in units:
        keys, values = heads[number]
        scores[number, pair] = mm_nt(q_ref[rows[number], columns[pair]], pair_operand(keys, pair))
        d_probs[number, pair] = mm_nt(dmix_ref[rows[number], columns[pair]], pair_operand(values, pair))
    probs, d_scores = {}, {}
    for unit in units:
        soft = soft_rows(scores[unit], allowed)
        probs[unit] = joined(soft).astype(BF16)
        d_soft = []
        for side, part in enumerate(soft):
            d_part = d_probs[unit][:, side * BLOCK : (side + 1) * BLOCK]
            d_soft.append(part * (d_part - jnp.sum(d_part * part, axis=-1, keepdims=True)))
        d_scores[unit] = joined(d_soft).astype(BF16)
    d_query, d_key_pair, d_value_pair = {}, {}, {}
    for number, pair in units:
        keys, _ = heads[number]
        d_query[number, pair] = mm(d_scores[number, pair], pair_operand(keys, pair))
        d_key_pair[number, pair] = mm_tn(d_scores[number, pair], q_ref[rows[number], columns[pair]])
        d_value_pair[number, pair] = mm_tn(probs[number, pair], dmix_ref[rows[number], columns[pair]])

    def collected(pieces, number, head, to_low):
        sides = [None, None]
        for query_head in range(HEADS):
            if query_head * KVH // HEADS == head:
                pair, side = divmod(query_head, 2)
                piece = pieces[number, pair][side * BLOCK : (side + 1) * BLOCK]
                sides[side] = piece if sides[side] is None else sides[side] + piece
        keep, move = (sides[0], sides[1]) if to_low else (sides[1], sides[0])
        total = keep if move is None else keep + pltpu.roll(move, HD, 1)
        return total

    for number in blocks:
        cosine = cos_ref[rows[number], :]
        sine = sin_ref[rows[number], :]
        sine = jnp.where(first_half, sine, -sine)

        def rope_back(grad):
            return grad * cosine + swapped(grad, first_half) * sine

        to = pl.ds(number * BLOCK, BLOCK)
        for pair in range(PAIRS):
            dq_ref[to, columns[pair]] = rope_back(d_query[number, pair] * HD ** (-0.5)).astype(BF16)
        key = [collected(d_key_pair, number, head, head % 2 == 0) for head in range(KVH)]
        value = [collected(d_value_pair, number, head, head % 2 == 1) for head in range(KVH)]
        dkv_ref[to, :128] = rope_back(jnp.where(low, key[0], key[1])).astype(BF16)
        dkv_ref[to, 128:256] = jnp.where(low, rope_back(key[2]), value[0]).astype(BF16)
        dkv_ref[to, 256:] = jnp.where(low, value[1], value[2]).astype(BF16)


def input_backward_kernel(n_shard, n_rep, idx, x_ref, nrm_ref, gain_ref, wq_full, wkv_full, dmid_ref, gout_ref,
                          gain_mlp_ref, dq_one, dq_two, dkv_one, dkv_two, din_ref, a_lo, a_hi, a_all, dq_all, dkv_all):
    model = x_ref.shape[1]
    width = gout_ref.shape[0]
    half_rows = dq_one.shape[0]
    dq_all[:half_rows, :] = dq_one[...]
    dq_all[half_rows:, :] = dq_two[...]
    dkv_all[:half_rows, :] = dkv_one[...]
    dkv_all[half_rows:, :] = dkv_two[...]
    own_normed = mm(nrm_ref[...], own_columns(idx[0], model, width)).astype(BF16)
    kv_width = dkv_all.shape[1]
    a_all[:width, :] = mm_tn(own_normed, dq_all[:, :model])
    a_all[width : 2 * width, :] = gout_ref[...]
    a_all[2 * width : 3 * width, :kv_width] = mm_tn(own_normed, dkv_all[...])
    a_all[2 * width : 3 * width, kv_width:] = jnp.zeros((width, model - kv_width), F32)
    d_normed = mm_nt(dq_all[...], wq_full[...]) + mm_nt(dkv_all[...], wkv_full[...])
    stream = x_ref[...].astype(F32)
    inv_attn = inverse_rms(stream)
    sum_attn = jnp.sum(d_normed * stream * inv_attn, axis=0, keepdims=True)
    tail = a_all.shape[0] - 3 * width
    row = lax.broadcasted_iota(jnp.int32, (tail, model), 0)
    a_all[3 * width :, :] = jnp.where(row == 0, sum_attn, jnp.where(row == 1, gain_mlp_ref[:1, :], 0.0))
    rows = a_all.shape[0] // n_rep
    middle = n_rep // 2
    for slab in range(n_rep):
        to = slab_place(idx[1] ^ slab, masks(n_rep, TURNED[2]))
        piece = a_all[slab * rows : (slab + 1) * rows, :].astype(BF16)

        @pl.when(to < middle)
        def _():
            a_lo[to] = piece

        @pl.when(to >= middle)
        def _():
            a_hi[to - middle] = piece

    own_in = d_normed[:BLOCK, :] * gain_ref[2:3, :]
    own_stream = stream[:BLOCK, :]
    own_inv = inv_attn[:BLOCK, :]
    din_ref[...] = (
        dmid_ref[...]
        + own_inv * own_in
        - own_inv**3 * own_stream * jnp.mean(own_in * own_stream, axis=-1, keepdims=True)
    ).T


def fetch(first, second, slab, steps, place):
    at = slab_place(slab, steps)
    middle = first.shape[0]

    @pl.when(at < middle)
    def _():
        place(first[at].astype(F32))

    @pl.when(at >= middle)
    def _():
        place(second[at - middle].astype(F32))


def unpack_mlp_kernel(n_rep, n_shard, idx, one_lo, one_hi, two_lo, two_hi, down_ref, gu_ref):
    shard = idx[0]
    member = idx[1]
    rows, chunk = two_lo.shape[1:]
    ff = gu_ref.shape[1] // 2
    groups = gu_ref.shape[0] // rows

    def place_gateup(slab, pair, piece):
        up, rest = divmod(slab, 2 * groups)
        column, group = divmod(rest, groups)
        base = ((shard ^ (2 * pair)) >> 1) * 2 * chunk + column * chunk + up * ff
        gu_ref[group * rows : (group + 1) * rows, pl.ds(pl.multiple_of(base, 128), chunk)] = piece

    def place_one(slab, piece):
        place_gateup(slab, 0, piece[:rows])
        down_ref[slab * rows : (slab + 1) * rows, :] = piece[rows:]

    for slab in range(n_rep):
        fetch(one_lo, one_hi, member ^ slab, masks(n_rep, TURNED[0]), functools.partial(place_one, slab))
        fetch(two_lo, two_hi, member ^ slab, masks(n_rep, TURNED[1]), functools.partial(place_gateup, slab, 1))


def unpack_attn_kernel(n_rep, idx, first, second, q_ref, kv_ref, o_ref, gain_ref, a_all):
    rows = first.shape[1]

    def place(slab, piece):
        a_all[slab * rows : (slab + 1) * rows, :] = piece

    for slab in range(n_rep):
        fetch(first, second, idx[1] ^ slab, masks(n_rep, TURNED[2]), functools.partial(place, slab))
    width = q_ref.shape[0]
    q_ref[...] = a_all[:width, :]
    o_ref[...] = a_all[width : 2 * width, :]
    kv_ref[...] = a_all[2 * width : 3 * width, : kv_ref.shape[1]]
    rows = a_all[3 * width :, :].astype(BF16)
    gain_ref[...] = mm(rows, own_columns(idx[0], rows.shape[1], width))


def call(body, operands, outs, scratch=(), micros=1, vmem=24, raw=()):
    in_vmem = pl.BlockSpec(memory_space=pltpu.VMEM)
    in_hbm = pl.BlockSpec(memory_space=pltpu.HBM)
    specs = [in_hbm if number in raw else in_vmem for number in range(1, len(operands))]
    return pl.pallas_call(
        body,
        out_shape=outs,
        in_specs=[pl.BlockSpec(memory_space=pltpu.SMEM)] + specs,
        out_specs=jax.tree.map(lambda _: in_vmem, outs),
        scratch_shapes=list(scratch),
        compiler_params=pltpu.CompilerParams(vmem_limit_bytes=vmem * 2**20),
        cost_estimate=pl.CostEstimate(flops=int(micros * 1e9), bytes_accessed=2**20, transcendentals=0),
    )(*operands)


def shape(dims, dtype):
    return jax.ShapeDtypeStruct(dims, dtype)


def exchange(value, axis, total, mask):
    return lax.ppermute(value, axis, [(member, member ^ mask) for member in range(total)])


def replica_steps(low, high, total, turned):
    steps = masks(total, turned)
    for mask in steps:
        arrived = exchange(high, "rep", total, mask)
        held = (low.astype(F32) + arrived.astype(F32)).astype(BF16)
        waited = yield held
        held = held if waited is None else after(held, *waited)
        low, high = held[: held.shape[0] // 2], held[held.shape[0] // 2 :]
    for mask in reversed(steps):
        arrived = exchange(held, "rep", total, mask)
        if mask == steps[0]:
            yield held, arrived
            return
        held = jnp.concatenate([held, arrived], axis=0)
        yield held


def last_of(steps):
    for result in steps:
        pass
    return result


def after(value, *earlier):
    return lax.optimization_barrier((value,) + earlier)[0]


def on_device(n_rep, n_shard, tokens, positions, seq_count, w_query, w_keyval, w_out, w_gateup, w_down, gain_attn,
              gain_mlp, out_grad):
    row_count, model = tokens.shape
    width = w_query.shape[1]
    ff = w_gateup.shape[2] // 2
    kv_width = w_keyval.shape[2]
    group_rows = n_shard * row_count
    shard = lax.axis_index("fsdp").astype(jnp.int32)
    member = lax.axis_index("rep").astype(jnp.int32)
    idx = jnp.stack([shard, member, seq_count[0]])
    pack_rows = 2 * width + width * kv_width // model
    own_full, half_full, gu_one, gu_two, cotangent = call(
        prepare_kernel,
        [idx, w_query[0], w_keyval[0], w_out[0], w_gateup[0], tokens.T, out_grad.T, positions[None], gain_attn,
         gain_mlp],
        (
            shape((pack_rows + row_count + 16, model), BF16),
            shape((pack_rows // 2 + row_count + 16, model), BF16),
            shape((width, ff // 2), BF16),
            shape((width, ff // 2), BF16),
            shape((row_count, model), BF16),
        ),
        [
            pltpu.VMEM((width, kv_width), BF16),
            pltpu.VMEM((model, row_count), BF16),
            pltpu.VMEM((model, row_count), BF16),
            pltpu.VMEM((16, model), F32),
            pltpu.SemaphoreType.DMA((7,)),
        ],
        micros=1,
        vmem=PREPARE_VMEM,
        raw=range(1, 7),
    )
    direct = exchange(half_full, "fsdp", n_shard, 2)
    direct_one = exchange(gu_one, "fsdp", n_shard, 2)
    around = exchange((direct[: pack_rows // 2]), "rep", n_rep, 1)
    packs = [own_full, exchange(own_full, "fsdp", n_shard, 1), direct, around,
             exchange(direct, "fsdp", n_shard, 1), exchange(around, "fsdp", n_shard, 1)]
    direct_two = exchange(gu_two, "fsdp", n_shard, 2)
    idx_late = after(idx, direct_one, direct_two)
    around_one = exchange(direct_one, "rep", n_rep, 1)
    around_two = exchange(direct_two, "rep", n_rep, 1)
    cot_across = exchange(cotangent, "fsdp", n_shard, 2)
    down_across = exchange(w_down[0].T, "fsdp", n_shard, 2)
    (x_all, normed, query, keyval, mixed, mid, normed_mid, cosine, sine, gains, wq_full, wkv_full, wo_full) = call(
        functools.partial(attn_forward_kernel, n_shard),
        [idx_late] + packs,
        (
            shape((group_rows, model), BF16),
            shape((group_rows, model), BF16),
            shape((group_rows, QW), BF16),
            shape((group_rows, kv_width), BF16),
            shape((group_rows, QW), BF16),
            shape((group_rows, model), F32),
            shape((group_rows, model), BF16),
            shape((group_rows, 128), F32),
            shape((group_rows, 128), F32),
            shape((16, model), F32),
            shape((model, QW), BF16),
            shape((model, kv_width), BF16),
            shape((QW, model), BF16),
        ),
        [
            pltpu.VMEM((group_rows, QW), F32),
            pltpu.VMEM((group_rows, kv_width), F32),
            pltpu.VMEM((n_shard, pack_rows, model), BF16),
            pltpu.VMEM((n_shard, 16, model), BF16),
            pltpu.SemaphoreType.DMA((6,)),
            pltpu.SemaphoreType.DMA((n_shard,)),
            pltpu.SemaphoreType.DMA((n_shard,)),
        ],
        micros=MICROS[0],
        raw=range(1, 7),
    )
    middle = n_rep // 2
    chunk = ff // n_shard
    slab_rows = width * 4 // n_rep
    a_rows = 3 * width + 16
    a_slab = (a_rows // n_rep, model)
    gu_beside = [exchange(piece, "fsdp", n_shard, 1) for piece in (w_gateup[0], direct_one, direct_two)]
    cot_own, down_own, cot_across, down_across, around_one, around_two, _ = lax.optimization_barrier(
        (cotangent, w_down[0].T, cot_across, down_across, around_one, around_two, gains)
    )
    around_beside = [exchange(piece, "fsdp", n_shard, 1) for piece in (around_one, around_two)]
    gu = [w_gateup[0], gu_beside[0], direct_one, direct_two, around_one, around_two] + gu_beside[1:] + around_beside
    cot = [cot_own, exchange(cot_own, "fsdp", n_shard, 1), cot_across, exchange(cot_across, "fsdp", n_shard, 1)]
    down_beside = exchange(down_own, "fsdp", n_shard, 1)
    half_act, half_dn, one_lo, one_hi, dcot, gu_full, own_mid = call(
        functools.partial(mlp_kernel, n_shard, n_rep, True),
        [idx, normed_mid, mid, down_own, down_beside] + cot + gu,
        (
            shape((row_count, model), F32),
            shape((group_rows, model), F32),
            shape((middle, 2 * slab_rows, chunk), BF16),
            shape((middle, 2 * slab_rows, chunk), BF16),
            shape((group_rows, model), BF16),
            shape((model, 2 * ff), BF16),
            shape((group_rows, width), BF16),
        ),
        [
            pltpu.VMEM((n_rep, 2 * slab_rows, chunk), BF16),
            pltpu.VMEM((model, 2 * chunk), BF16),
            pltpu.VMEM((group_rows, 2 * chunk), BF16),
            pltpu.SemaphoreType.DMA((10,)),
            pltpu.SemaphoreType.DMA((2,)),
            pltpu.SemaphoreType.DMA((n_shard,)),
        ],
        micros=MICROS[1],
        raw=range(3, 15 + n_shard),
    )
    down_across, _ = lax.optimization_barrier((down_across, half_act))
    down_corner = exchange(down_across, "fsdp", n_shard, 1)
    out_act, d_normed_mid, two_lo, two_hi = call(
        functools.partial(mlp_kernel, n_shard, n_rep, False),
        [idx, normed_mid, half_act, down_across, down_corner, dcot, gu_full, own_mid, half_dn],
        (
            shape((model, row_count), F32),
            shape((group_rows, model), F32),
            shape((middle, slab_rows, chunk), BF16),
            shape((middle, slab_rows, chunk), BF16),
        ),
        [
            pltpu.VMEM((n_rep, slab_rows, chunk), BF16),
            pltpu.VMEM((model, 2 * chunk), BF16),
            pltpu.SemaphoreType.DMA((2,)),
        ],
        micros=MICROS[2],
        raw=(3, 4),
    )
    one = replica_steps(one_lo, one_hi, n_rep, TURNED[0])
    two = replica_steps(two_lo, two_hi, n_rep, TURNED[1])
    d_attn, d_mixed, d_mid, part_out, part_gain = call(
        functools.partial(residual_backward_kernel, n_shard),
        [idx, mid, d_normed_mid, dcot, mixed, gains, wo_full],
        (
            shape((group_rows, model), BF16),
            shape((group_rows, QW), BF16),
            shape((row_count, model), F32),
            shape((width, model), F32),
            shape((8, model), F32),
        ),
        micros=MICROS[3],
    )
    reached = [0, 0]
    results = {}

    def advance(kernel):
        for chain, steps in enumerate((one, two)):
            while reached[chain] < TIES[kernel][chain]:
                results[chain] = next(steps)
                reached[chain] += 1
        return [results[chain] for chain in results]

    halves = []
    for first_row in (0, group_rows // 2):
        d_mixed = after(d_mixed, *advance(len(halves)), *(half[0] for half in halves))
        halves.append(
            call(
                functools.partial(heads_backward_kernel, first_row),
                [idx, query, keyval, d_mixed, cosine, sine],
                (shape((group_rows // 2, QW), BF16), shape((group_rows // 2, kv_width), BF16)),
                micros=MICROS[4],
            )
        )
    d_mid = after(d_mid, *advance(2))
    in_grad, a_lo, a_hi = call(
        functools.partial(input_backward_kernel, n_shard, n_rep),
        [idx, x_all, normed, gains, wq_full, wkv_full, d_mid, part_out, part_gain,
         halves[0][0], halves[1][0], halves[0][1], halves[1][1]],
        (
            shape((model, row_count), F32),
            shape((middle,) + a_slab, BF16),
            shape((middle,) + a_slab, BF16),
        ),
        [
            pltpu.VMEM((a_rows, model), F32),
            pltpu.VMEM((group_rows, QW), BF16),
            pltpu.VMEM((group_rows, kv_width), BF16),
        ],
        micros=MICROS[5],
    )
    one, two = last_of(one), last_of(two)
    attn = last_of(replica_steps(a_lo, a_hi, n_rep, TURNED[2]))
    grad_down, grad_gateup = call(
        functools.partial(unpack_mlp_kernel, n_rep, n_shard),
        [idx] + list(one) + list(two),
        (shape((model, chunk), F32), shape((width, 2 * ff), F32)),
        micros=3,
    )
    grad_query, grad_keyval, grad_out, own_gains = call(
        functools.partial(unpack_attn_kernel, n_rep),
        [idx] + list(attn),
        (
            shape((width, model), F32),
            shape((width, kv_width), F32),
            shape((width, model), F32),
            shape((a_rows - 3 * width, width), F32),
        ),
        [pltpu.VMEM((a_rows, model), F32)],
        micros=2,
    )
    return (
        out_act.T,
        in_grad.T,
        grad_query[None],
        grad_keyval[None],
        grad_out[None],
        grad_gateup[None],
        grad_down.T[None],
        own_gains[:1],
        own_gains[1:2],
    )


def solution(mesh):
    placed = (
        P(("rep", "fsdp"), None),
        P(("rep", "fsdp")),
        P(("rep", "fsdp")),
        P(None, "fsdp", None),
        P(None, "fsdp", None),
        P(None, "fsdp", None),
        P(None, "fsdp", None),
        P(None, "fsdp", None),
        P(None, "fsdp"),
        P(None, "fsdp"),
        P(("rep", "fsdp"), None),
    )
    return jax.shard_map(
        functools.partial(on_device, mesh.shape["rep"], mesh.shape["fsdp"]),
        mesh=mesh,
        in_specs=placed,
        out_specs=(
            P(("rep", "fsdp"), None),
            P(("rep", "fsdp"), None),
            P(None, "fsdp", None),
            P(None, "fsdp", None),
            P(None, "fsdp", None),
            P(None, "fsdp", None),
            P(None, "fsdp", None),
            P(None, "fsdp"),
            P(None, "fsdp"),
        ),
        check_vma=False,
    )
```

```python
import functools

import jax
import jax.numpy as jnp
from jax import lax
from jax.experimental import pallas as pl
from jax.experimental.pallas import tpu as pltpu
from jax.sharding import PartitionSpec as P

HEADS = 9
KVH = 3
HD = 64
LEN = 64
norm_eps = 1e-05
rope_base = 100000.0

BLOCK = 128
PAIRS = 5
QW = PAIRS * 128
GROUP = 4
PREPARE_VMEM = 60
TURNED = (0, 0, 0)
TIES = ((1, 0), (1, 1), (2, 1))
MICROS = (1, 6, 6, 3, 4, 4)
F32 = jnp.float32
BF16 = jnp.bfloat16


def mm(left, right):
    return jnp.dot(left, right, preferred_element_type=F32)


def mm_nt(left, right):
    return lax.dot_general(left, right, (((1,), (1,)), ((), ())), preferred_element_type=F32)


def mm_tn(left, right):
    return lax.dot_general(left, right, (((0,), (0,)), ((), ())), preferred_element_type=F32)


def inverse_rms(stream):
    return lax.rsqrt(jnp.mean(stream * stream, axis=-1, keepdims=True) + norm_eps)


def lane_index(shape):
    return lax.broadcasted_iota(jnp.int32, shape, 1)


def own_columns(shard, rows, width):
    row = lax.broadcasted_iota(jnp.int32, (rows, width), 0)
    column = lax.broadcasted_iota(jnp.int32, (rows, width), 1)
    return (row == column + shard * width).astype(BF16)


def swapped(values, first_half):
    return jnp.where(first_half, pltpu.roll(values, 96, 1), pltpu.roll(values, 32, 1))


def split_heads(keyval):
    low = lane_index((BLOCK, 128)) < HD
    slices = [keyval[:, 128 * part : 128 * part + 128].astype(F32) for part in range(3)]

    def pair(piece, is_low):
        kept = jnp.where(low, piece, 0.0) if is_low else jnp.where(low, 0.0, piece)
        moved = pltpu.roll(kept, HD, 1)
        kept, moved = kept.astype(BF16), moved.astype(BF16)
        return (kept, moved) if is_low else (moved, kept)

    keys = [pair(slices[0], True), pair(slices[0], False), pair(slices[1], True)]
    values = [pair(slices[1], False), pair(slices[2], True), pair(slices[2], False)]
    return keys, values


def pair_operand(parts, pair):
    first = parts[(2 * pair) * KVH // HEADS][0]
    if 2 * pair + 1 >= HEADS:
        return first
    return jnp.concatenate([first, parts[(2 * pair + 1) * KVH // HEADS][1]], axis=0)


def attention_mask():
    query = lax.broadcasted_iota(jnp.int32, (BLOCK, BLOCK), 0)
    key = lax.broadcasted_iota(jnp.int32, (BLOCK, BLOCK), 1)
    return (query // LEN == key // LEN) & (query >= key)


def soft_rows(scores, allowed):
    halves = []
    for start in range(0, scores.shape[1], BLOCK):
        part = jnp.where(allowed, scores[:, start : start + BLOCK], -1e30)
        part = jnp.exp(part - jnp.max(part, axis=-1, keepdims=True))
        halves.append(part * (1.0 / jnp.sum(part, axis=-1, keepdims=True)))
    return halves


def joined(halves):
    return halves[0] if len(halves) == 1 else jnp.concatenate(halves, axis=1)


def prepare_kernel(idx, wq, wkv, wo, wgu, tokens, grad, positions, gain_attn, gain_mlp,
                   own_ref, send_ref, gu_one, gu_two, cot_ref, kv_all, tok_all, grad_all, codes, sem):
    width, kv_width = wkv.shape
    model = own_ref.shape[1]
    side = idx[1] & 1
    part = gu_one.shape[1]
    across = [pl.ds(pl.multiple_of((2 * side + number) * part, 128), part) for number in range(2)]
    waits = [
        pltpu.make_async_copy(wkv, kv_all, sem.at[0]),
        pltpu.make_async_copy(wq, own_ref.at[pl.ds(0, width)], sem.at[1]),
        pltpu.make_async_copy(wo, own_ref.at[pl.ds(width, width)], sem.at[2]),
        pltpu.make_async_copy(tokens, tok_all, sem.at[3]),
        pltpu.make_async_copy(grad, grad_all, sem.at[4]),
        pltpu.make_async_copy(wgu.at[:, across[0]], gu_one, sem.at[5]),
        pltpu.make_async_copy(wgu.at[:, across[1]], gu_two, sem.at[6]),
    ]
    for wait in waits:
        wait.start()
    count = send_ref.shape[0] - BLOCK - 16
    codes[...] = jnp.zeros_like(codes)
    codes[0:1, :BLOCK] = (positions[...] >> 6).astype(F32)
    codes[1:2, :BLOCK] = (positions[...] & 63).astype(F32)
    codes[2:3, :width] = gain_attn[...].astype(F32)
    codes[3:4, :width] = gain_mlp[...].astype(F32)
    small = codes[...].astype(BF16)
    own_ref[2 * count + BLOCK :, :] = small
    send_ref[count + BLOCK :, :] = small
    rest = model - kv_width
    top = width - width * rest // model
    waits[0].wait()
    own_ref[2 * width : 2 * count, :kv_width] = kv_all[:top, :]
    own_ref[2 * width : 3 * width - top, kv_width:] = kv_all[top:, :rest]
    own_ref[3 * width - top : 2 * count, kv_width:] = kv_all[top:, rest:]
    waits[3].wait()
    rows = tok_all[...].T
    own_ref[2 * count : 2 * count + BLOCK, :] = rows
    send_ref[count : count + BLOCK, :] = rows
    waits[1].wait()
    waits[2].wait()
    send_ref[:count, :] = own_ref[pl.ds(pl.multiple_of(side * count, 16), count), :]
    waits[4].wait()
    cot_ref[...] = (grad_all[...].T.astype(F32) * live_rows(idx)).astype(BF16)
    waits[5].wait()
    waits[6].wait()


def live_rows(idx):
    slot = lax.broadcasted_iota(jnp.int32, (BLOCK, 1), 0) // LEN
    return (slot < idx[2]).astype(F32)


def attn_forward_kernel(n_shard, idx, *refs):
    packs = refs[:6]
    (x_ref, nrm_ref, q_ref, kv_ref, mix_ref, mid_ref, nmid_ref, cos_ref, sin_ref, gain_ref,
     wq_full, wkv_full, wo_full, query_all, keyval_all, pack_all, small, sem, tok_sem, small_sem) = refs[6:]
    shard = idx[0]
    side = idx[1] & 1
    model = x_ref.shape[1]
    width = model // n_shard
    count = pack_all.shape[1] // 2
    waits = []
    pieces = [(0, packs[0], None), (1, packs[1], None), (2, packs[2], side), (2, packs[3], 1 - side),
              (3, packs[4], side), (3, packs[5], 1 - side)]
    for number, (part, source, which) in enumerate(pieces):
        target = pack_all.at[part]
        size = 2 * count
        if which is not None:
            target = pack_all.at[part, pl.ds(pl.multiple_of(which * count, 16), count)]
            size = count
        waits.append(pltpu.make_async_copy(source.at[pl.ds(0, size)], target, sem.at[number]))
        if number not in (3, 5):
            tokens_to = x_ref.at[pl.ds(part * BLOCK, BLOCK)]
            waits.append(pltpu.make_async_copy(source.at[pl.ds(size, BLOCK)], tokens_to, tok_sem.at[part]))
            rest = source.at[pl.ds(size + BLOCK, 16)]
            waits.append(pltpu.make_async_copy(rest, small.at[part], small_sem.at[part]))
    for wait in waits:
        wait.start()
    wq_full[:, model:] = jnp.zeros((model, QW - model), BF16)
    wo_full[model:, :] = jnp.zeros((QW - model, model), BF16)
    for wait in waits:
        wait.wait()
    gains = jnp.zeros((16, model), F32)
    kv_width = wkv_full.shape[1]
    rest = model - kv_width
    top = width - width * rest // model
    for part in range(n_shard):
        at = pl.multiple_of((shard ^ part) * width, 16)
        wq_full[pl.ds(at, width), :model] = pack_all[part, :width, :]
        wo_full[pl.ds(at, width), :] = pack_all[part, width : 2 * width, :]
        wkv_full[pl.ds(at, top), :] = pack_all[part, 2 * width :, :kv_width]
        low = pl.ds(pl.multiple_of(at + top, 16), width - top)
        wkv_full[low, :rest] = pack_all[part, 2 * width : 3 * width - top, model - rest :]
        wkv_full[low, rest:] = pack_all[part, 3 * width - top :, model - rest :]
        row = lax.broadcasted_iota(jnp.int32, (256, model), 0)
        column = lax.broadcasted_iota(jnp.int32, (256, model), 1)
        place = ((column == row + at) & (row < width)).astype(BF16)
        gains = gains + mm(small[part, :, :256], place)
    gain_ref[...] = gains
    half = HD // 2
    step = lax.broadcasted_iota(jnp.int32, (half, 1), 0).astype(F32)
    frequency = jnp.exp(step * (-2.0 / HD * jnp.log(F32(rope_base))))
    for part in range(n_shard):
        codes = small[part].astype(F32)
        position = codes[0:1, :BLOCK] * 64.0 + codes[1:2, :BLOCK]
        angle = frequency * position
        rows = pl.ds(part * BLOCK, BLOCK)
        cos_ref[rows, :] = jnp.concatenate([jnp.cos(angle)] * 4, axis=0).T
        sin_ref[rows, :] = jnp.concatenate([jnp.sin(angle)] * 4, axis=0).T
    allowed = attention_mask()
    lane = lane_index((BLOCK, 128))
    first_half = lane % HD < half
    gain_attn = gains[2:3, :]
    gain_mlp = gains[3:4, :]

    for part in range(n_shard):
        rows = pl.ds(part * BLOCK, BLOCK)
        stream = x_ref[rows, :].astype(F32)
        nrm_ref[rows, :] = (stream * inverse_rms(stream) * gain_attn).astype(BF16)
    query_all[...] = mm(nrm_ref[...], wq_full[...])
    keyval_all[...] = mm(nrm_ref[...], wkv_full[...])

    heads = []
    for number in range(n_shard):
        rows = pl.ds(number * BLOCK, BLOCK)
        cosine = cos_ref[rows, :]
        sine = sin_ref[rows, :]
        sine = jnp.where(first_half, -sine, sine)

        def rope(values):
            return values * cosine + swapped(values, first_half) * sine

        kv_ref[rows, :128] = rope(keyval_all[rows, :128]).astype(BF16)
        second = keyval_all[rows, 128:256]
        kv_ref[rows, 128:256] = jnp.where(lane < HD, rope(second), second).astype(BF16)
        kv_ref[rows, 256:] = keyval_all[rows, 256:].astype(BF16)
        for pair in range(PAIRS):
            columns = slice(128 * pair, 128 * pair + 128)
            q_ref[rows, columns] = (rope(query_all[rows, columns]) * HD ** (-0.5)).astype(BF16)
        heads.append(split_heads(kv_ref[rows, :]))
    for start in range(0, n_shard, GROUP):
        units = [(number, pair) for number in range(start, start + GROUP) for pair in range(PAIRS)]
        scores, probs = {}, {}
        for number, pair in units:
            query = q_ref[number * BLOCK : (number + 1) * BLOCK, 128 * pair : 128 * pair + 128]
            scores[number, pair] = mm_nt(query, pair_operand(heads[number][0], pair))
        for unit in units:
            probs[unit] = joined(soft_rows(scores[unit], allowed)).astype(BF16)
        for number, pair in units:
            mixed = mm(probs[number, pair], pair_operand(heads[number][1], pair))
            mix_ref[number * BLOCK : (number + 1) * BLOCK, 128 * pair : 128 * pair + 128] = mixed.astype(BF16)
    stream_mid = x_ref[...].astype(F32) + mm(mix_ref[...], wo_full[...])
    mid_ref[...] = stream_mid
    nmid_ref[...] = (stream_mid * inverse_rms(stream_mid) * gain_mlp).astype(BF16)


def masks(total, turned):
    steps = []
    while 2 ** len(steps) < total:
        steps.append(2 ** len(steps))
    return steps[turned:] + steps[:turned]


def slab_place(value, steps):
    result = jnp.zeros_like(value)
    for mask in steps:
        result = result * 2 + ((value & mask) != 0).astype(jnp.int32)
    return result


def spread(target, member, steps, first_row, slab, value):
    to = slab_place(member ^ slab, steps)
    target[to, first_row : first_row + value.shape[0], :] = value.astype(BF16)


def mlp_kernel(n_shard, n_rep, first_call, idx, *refs):
    if first_call:
        (nmid_ref, mid_ref, wd_own, wd_other), cot, wgu = refs[:4], refs[4 : 4 + n_shard], refs[4 + n_shard : -13]
        (act_ref, dn_ref, lo_ref, hi_ref, dcot_ref, w_full, own_ref, all_ref, wd_pair, wide_ref, sem, wd_sem,
         cot_sem) = refs[-13:]
    else:
        (nmid_ref, act_in, wd_own, wd_other, dcot_ref, w_full, own_ref, dn_in, act_ref, dn_ref, lo_ref,
         hi_ref, all_ref, wd_pair, wd_sem) = refs
    shard = idx[0]
    member = idx[1]
    first = 0 if first_call else 2
    steps = masks(n_rep, TURNED[0] if first_call else TURNED[1])
    model = nmid_ref.shape[1]
    ff = w_full.shape[1] // 2
    chunk = ff // n_shard
    waits = []
    for part, source in ((first, wd_own), (first + 1, wd_other)):
        at = pl.multiple_of(((shard ^ part) & 1) * chunk, 128)
        waits.append(pltpu.make_async_copy(source, wd_pair.at[:, pl.ds(at, chunk)], wd_sem.at[part - first]))
    if first_call:
        width = model // n_shard
        side = member & 1
        pieces = [(0, wgu[0], None), (1, wgu[1], None)]
        for number in range(8):
            part, rest = divmod(number, 4)
            which = side if rest < 2 else 1 - side
            pieces.append((2 + part, wgu[2 + number], 2 * which + rest % 2))
        for number, (part, source, which) in enumerate(pieces):
            down = pl.ds(pl.multiple_of((shard ^ part) * width, 16), width)
            if which is None:
                target = w_full.at[down]
            else:
                size = ff // 2
                target = w_full.at[down, pl.ds(pl.multiple_of(which * size, 128), size)]
            waits.append(pltpu.make_async_copy(source, target, sem.at[number]))
        for part in range(n_shard):
            waits.append(
                pltpu.make_async_copy(cot[part], dcot_ref.at[pl.ds(part * BLOCK, BLOCK)], cot_sem.at[part])
            )
    for wait in waits:
        wait.start()
    if first_call:
        own_ref[...] = mm(nmid_ref[...], own_columns(shard, model, width)).astype(BF16)
    for wait in waits:
        wait.wait()
    normed_mid = nmid_ref[...]
    d_branch = dcot_ref[...]
    base = ((shard ^ first) >> 1) * 2 * chunk
    gate_at = pl.ds(pl.multiple_of(base, 256), 2 * chunk)
    up_at = pl.ds(pl.multiple_of(base + ff, 256), 2 * chunk)
    gate = mm(normed_mid, w_full[:, gate_at])
    up = mm(normed_mid, w_full[:, up_at])
    d_hidden = mm(d_branch, wd_pair[...])
    sigmoid = 0.5 * jnp.tanh(0.5 * gate) + 0.5
    silu = gate * sigmoid
    hidden = (silu * up).astype(BF16)
    d_gate = (d_hidden * up * sigmoid * (1.0 + gate * (1.0 - sigmoid))).astype(BF16)
    d_up = (d_hidden * silu).astype(BF16)
    rows = all_ref.shape[1]
    if first_call:
        wide_ref[...] = hidden
        own_hidden = wide_ref[:, pl.ds(pl.multiple_of((shard & 1) * chunk, 128), chunk)]
        rows = rows // 2
        grad_down = mm_tn(d_branch, own_hidden)
        for slab in range(n_rep):
            spread(all_ref, member, steps, rows, slab, grad_down[slab * rows : (slab + 1) * rows])
    slab = 0
    for piece in (d_gate, d_up):
        grad = mm_tn(own_ref[...], piece)
        for column in range(0, 2 * chunk, chunk):
            for row in range(0, grad.shape[0], rows):
                spread(all_ref, member, steps, 0, slab, grad[row : row + rows, column : column + chunk])
                slab += 1
    middle = n_rep // 2
    lo_ref[...] = all_ref[:middle]
    hi_ref[...] = all_ref[middle:]
    d_normed = mm_nt(d_gate, w_full[:, gate_at]) + mm_nt(d_up, w_full[:, up_at])
    added = mm_nt(hidden[:BLOCK], wd_pair[...])
    if first_call:
        dn_ref[...] = d_normed
        act_ref[...] = mid_ref[:BLOCK, :] + added
    else:
        dn_ref[...] = dn_in[...] + d_normed
        act_ref[...] = ((act_in[...] + added) * live_rows(idx)).T


def residual_backward_kernel(n_shard, idx, mid_ref, dn_ref, dcot_ref, mix_ref, gain_ref, wo_full,
                             dattn_ref, dmix_ref, dmid_ref, gout_ref, gain_out):
    model = mid_ref.shape[1]
    stream_mid = mid_ref[...]
    inv_mlp = inverse_rms(stream_mid)
    d_normed_mid = dn_ref[...]
    sum_mlp = jnp.sum(d_normed_mid * stream_mid * inv_mlp, axis=0, keepdims=True)
    scaled = d_normed_mid * gain_ref[3:4, :]
    d_mid = (
        dcot_ref[...].astype(F32)
        + inv_mlp * scaled
        - inv_mlp**3 * stream_mid * jnp.mean(scaled * stream_mid, axis=-1, keepdims=True)
    )
    dmid_ref[...] = d_mid[:BLOCK, :]
    dattn_ref[...] = d_mid.astype(BF16)
    dmix_ref[...] = mm_nt(dattn_ref[...], wo_full[...]).astype(BF16)
    own_mixed = mm(mix_ref[:, :model], own_columns(idx[0], model, gout_ref.shape[0])).astype(BF16)
    gout_ref[...] = mm_tn(own_mixed, dattn_ref[...])
    gain_out[...] = jnp.broadcast_to(sum_mlp, gain_out.shape)


def heads_backward_kernel(first_row, idx, q_ref, kv_ref, dmix_ref, cos_ref, sin_ref, dq_ref, dkv_ref):
    half = HD // 2
    allowed = attention_mask()
    lane = lane_index((BLOCK, 128))
    first_half = lane % HD < half
    low = lane < HD
    blocks = range(dq_ref.shape[0] // BLOCK)
    units = [(number, pair) for number in blocks for pair in range(PAIRS)]
    rows = [pl.ds(first_row + number * BLOCK, BLOCK) for number in blocks]
    columns = [slice(128 * pair, 128 * pair + 128) for pair in range(PAIRS)]
    heads = [split_heads(kv_ref[rows[number], :]) for number in blocks]
    scores, d_probs = {}, {}
    for number, pair in units:
        keys, values = heads[number]
        scores[number, pair] = mm_nt(q_ref[rows[number], columns[pair]], pair_operand(keys, pair))
        d_probs[number, pair] = mm_nt(dmix_ref[rows[number], columns[pair]], pair_operand(values, pair))
    probs, d_scores = {}, {}
    for unit in units:
        soft = soft_rows(scores[unit], allowed)
        probs[unit] = joined(soft).astype(BF16)
        d_soft = []
        for side, part in enumerate(soft):
            d_part = d_probs[unit][:, side * BLOCK : (side + 1) * BLOCK]
            d_soft.append(part * (d_part - jnp.sum(d_part * part, axis=-1, keepdims=True)))
        d_scores[unit] = joined(d_soft).astype(BF16)
    d_query, d_key_pair, d_value_pair = {}, {}, {}
    for number, pair in units:
        keys, _ = heads[number]
        d_query[number, pair] = mm(d_scores[number, pair], pair_operand(keys, pair))
        d_key_pair[number, pair] = mm_tn(d_scores[number, pair], q_ref[rows[number], columns[pair]])
        d_value_pair[number, pair] = mm_tn(probs[number, pair], dmix_ref[rows[number], columns[pair]])

    def collected(pieces, number, head, to_low):
        sides = [None, None]
        for query_head in range(HEADS):
            if query_head * KVH // HEADS == head:
                pair, side = divmod(query_head, 2)
                piece = pieces[number, pair][side * BLOCK : (side + 1) * BLOCK]
                sides[side] = piece if sides[side] is None else sides[side] + piece
        keep, move = (sides[0], sides[1]) if to_low else (sides[1], sides[0])
        total = keep if move is None else keep + pltpu.roll(move, HD, 1)
        return total

    for number in blocks:
        cosine = cos_ref[rows[number], :]
        sine = sin_ref[rows[number], :]
        sine = jnp.where(first_half, sine, -sine)

        def rope_back(grad):
            return grad * cosine + swapped(grad, first_half) * sine

        to = pl.ds(number * BLOCK, BLOCK)
        for pair in range(PAIRS):
            dq_ref[to, columns[pair]] = rope_back(d_query[number, pair] * HD ** (-0.5)).astype(BF16)
        key = [collected(d_key_pair, number, head, head % 2 == 0) for head in range(KVH)]
        value = [collected(d_value_pair, number, head, head % 2 == 1) for head in range(KVH)]
        dkv_ref[to, :128] = rope_back(jnp.where(low, key[0], key[1])).astype(BF16)
        dkv_ref[to, 128:256] = jnp.where(low, rope_back(key[2]), value[0]).astype(BF16)
        dkv_ref[to, 256:] = jnp.where(low, value[1], value[2]).astype(BF16)


def input_backward_kernel(n_shard, n_rep, idx, x_ref, nrm_ref, gain_ref, wq_full, wkv_full, dmid_ref, gout_ref,
                          gain_mlp_ref, dq_one, dq_two, dkv_one, dkv_two, din_ref, a_lo, a_hi, a_all, dq_all, dkv_all):
    model = x_ref.shape[1]
    width = gout_ref.shape[0]
    half_rows = dq_one.shape[0]
    dq_all[:half_rows, :] = dq_one[...]
    dq_all[half_rows:, :] = dq_two[...]
    dkv_all[:half_rows, :] = dkv_one[...]
    dkv_all[half_rows:, :] = dkv_two[...]
    own_normed = mm(nrm_ref[...], own_columns(idx[0], model, width)).astype(BF16)
    kv_width = dkv_all.shape[1]
    a_all[:width, :] = mm_tn(own_normed, dq_all[:, :model])
    a_all[width : 2 * width, :] = gout_ref[...]
    a_all[2 * width : 3 * width, :kv_width] = mm_tn(own_normed, dkv_all[...])
    a_all[2 * width : 3 * width, kv_width:] = jnp.zeros((width, model - kv_width), F32)
    d_normed = mm_nt(dq_all[...], wq_full[...]) + mm_nt(dkv_all[...], wkv_full[...])
    stream = x_ref[...].astype(F32)
    inv_attn = inverse_rms(stream)
    sum_attn = jnp.sum(d_normed * stream * inv_attn, axis=0, keepdims=True)
    tail = a_all.shape[0] - 3 * width
    row = lax.broadcasted_iota(jnp.int32, (tail, model), 0)
    a_all[3 * width :, :] = jnp.where(row == 0, sum_attn, jnp.where(row == 1, gain_mlp_ref[:1, :], 0.0))
    rows = a_all.shape[0] // n_rep
    middle = n_rep // 2
    for slab in range(n_rep):
        to = slab_place(idx[1] ^ slab, masks(n_rep, TURNED[2]))
        piece = a_all[slab * rows : (slab + 1) * rows, :].astype(BF16)

        @pl.when(to < middle)
        def _():
            a_lo[to] = piece

        @pl.when(to >= middle)
        def _():
            a_hi[to - middle] = piece

    own_in = d_normed[:BLOCK, :] * gain_ref[2:3, :]
    own_stream = stream[:BLOCK, :]
    own_inv = inv_attn[:BLOCK, :]
    din_ref[...] = (
        dmid_ref[...]
        + own_inv * own_in
        - own_inv**3 * own_stream * jnp.mean(own_in * own_stream, axis=-1, keepdims=True)
    ).T


def fetch(first, second, slab, steps, place):
    at = slab_place(slab, steps)
    middle = first.shape[0]

    @pl.when(at < middle)
    def _():
        place(first[at].astype(F32))

    @pl.when(at >= middle)
    def _():
        place(second[at - middle].astype(F32))


def unpack_mlp_kernel(n_rep, n_shard, idx, one_lo, one_hi, two_lo, two_hi, gu_ref):
    shard = idx[0]
    member = idx[1]
    rows, chunk = two_lo.shape[1:]
    ff = gu_ref.shape[1] // 2
    groups = gu_ref.shape[0] // rows

    def place_gateup(slab, pair, piece):
        up, rest = divmod(slab, 2 * groups)
        column, group = divmod(rest, groups)
        base = ((shard ^ (2 * pair)) >> 1) * 2 * chunk + column * chunk + up * ff
        gu_ref[group * rows : (group + 1) * rows, pl.ds(pl.multiple_of(base, 128), chunk)] = piece

    def place_one(slab, piece):
        place_gateup(slab, 0, piece[:rows])

    for slab in range(n_rep):
        fetch(one_lo, one_hi, member ^ slab, masks(n_rep, TURNED[0]), functools.partial(place_one, slab))
        fetch(two_lo, two_hi, member ^ slab, masks(n_rep, TURNED[1]), functools.partial(place_gateup, slab, 1))


def unpack_down_kernel(n_rep, idx, first, second, down_ref):
    rows = first.shape[1] // 2

    def place(slab, piece):
        down_ref[slab * rows : (slab + 1) * rows, :] = piece[rows:]

    for slab in range(n_rep):
        fetch(first, second, idx[1] ^ slab, masks(n_rep, TURNED[0]), functools.partial(place, slab))


def unpack_attn_kernel(n_rep, idx, first, second, q_ref, kv_ref, o_ref, gain_attn_ref, gain_mlp_ref, a_all):
    rows = first.shape[1]

    def place(slab, piece):
        a_all[slab * rows : (slab + 1) * rows, :] = piece

    for slab in range(n_rep):
        fetch(first, second, idx[1] ^ slab, masks(n_rep, TURNED[2]), functools.partial(place, slab))
    width = q_ref.shape[0]
    q_ref[...] = a_all[:width, :]
    o_ref[...] = a_all[width : 2 * width, :]
    kv_ref[...] = a_all[2 * width : 3 * width, : kv_ref.shape[1]]
    rows = a_all[3 * width :, :].astype(BF16)
    own = mm(rows, own_columns(idx[0], rows.shape[1], width))
    gain_attn_ref[...] = own[0:1]
    gain_mlp_ref[...] = own[1:2]


def call(body, operands, outs, scratch=(), micros=1, vmem=24, raw=()):
    in_vmem = pl.BlockSpec(memory_space=pltpu.VMEM)
    in_hbm = pl.BlockSpec(memory_space=pltpu.HBM)
    specs = [in_hbm if number in raw else in_vmem for number in range(1, len(operands))]
    return pl.pallas_call(
        body,
        out_shape=outs,
        in_specs=[pl.BlockSpec(memory_space=pltpu.SMEM)] + specs,
        out_specs=jax.tree.map(lambda _: in_vmem, outs),
        scratch_shapes=list(scratch),
        compiler_params=pltpu.CompilerParams(vmem_limit_bytes=vmem * 2**20),
        cost_estimate=pl.CostEstimate(flops=int(micros * 1e9), bytes_accessed=2**20, transcendentals=0),
    )(*operands)


def shape(dims, dtype):
    return jax.ShapeDtypeStruct(dims, dtype)


def exchange(value, axis, total, mask):
    return lax.ppermute(value, axis, [(member, member ^ mask) for member in range(total)])


def replica_steps(low, high, total, turned):
    steps = masks(total, turned)
    for mask in steps:
        arrived = exchange(high, "rep", total, mask)
        held = (low.astype(F32) + arrived.astype(F32)).astype(BF16)
        waited = yield held
        held = held if waited is None else after(held, *waited)
        low, high = held[: held.shape[0] // 2], held[held.shape[0] // 2 :]
    for mask in reversed(steps):
        arrived = exchange(held, "rep", total, mask)
        if mask == steps[0]:
            yield held, arrived
            return
        held = jnp.concatenate([held, arrived], axis=0)
        yield held


def last_of(steps):
    for result in steps:
        pass
    return result


def after(value, *earlier):
    return lax.optimization_barrier((value,) + earlier)[0]


def on_device(n_rep, n_shard, tokens, positions, seq_count, w_query, w_keyval, w_out, w_gateup, w_down, gain_attn,
              gain_mlp, out_grad):
    row_count, model = tokens.shape
    width = w_query.shape[1]
    ff = w_gateup.shape[2] // 2
    kv_width = w_keyval.shape[2]
    group_rows = n_shard * row_count
    shard = lax.axis_index("fsdp").astype(jnp.int32)
    member = lax.axis_index("rep").astype(jnp.int32)
    idx = jnp.stack([shard, member, seq_count[0]])
    pack_rows = 2 * width + width * kv_width // model
    own_full, half_full, gu_one, gu_two, cotangent = call(
        prepare_kernel,
        [idx, w_query[0], w_keyval[0], w_out[0], w_gateup[0], tokens.T, out_grad.T, positions[None], gain_attn,
         gain_mlp],
        (
            shape((pack_rows + row_count + 16, model), BF16),
            shape((pack_rows // 2 + row_count + 16, model), BF16),
            shape((width, ff // 2), BF16),
            shape((width, ff // 2), BF16),
            shape((row_count, model), BF16),
        ),
        [
            pltpu.VMEM((width, kv_width), BF16),
            pltpu.VMEM((model, row_count), BF16),
            pltpu.VMEM((model, row_count), BF16),
            pltpu.VMEM((16, model), F32),
            pltpu.SemaphoreType.DMA((7,)),
        ],
        micros=1,
        vmem=PREPARE_VMEM,
        raw=range(1, 7),
    )
    direct = exchange(half_full, "fsdp", n_shard, 2)
    direct_one = exchange(gu_one, "fsdp", n_shard, 2)
    around = exchange((direct[: pack_rows // 2]), "rep", n_rep, 1)
    packs = [own_full, exchange(own_full, "fsdp", n_shard, 1), direct, around,
             exchange(direct, "fsdp", n_shard, 1), exchange(around, "fsdp", n_shard, 1)]
    direct_two = exchange(gu_two, "fsdp", n_shard, 2)
    idx_late = after(idx, direct_one, direct_two)
    around_one = exchange(direct_one, "rep", n_rep, 1)
    around_two = exchange(direct_two, "rep", n_rep, 1)
    cot_across = exchange(cotangent, "fsdp", n_shard, 2)
    down_across = exchange(w_down[0].T, "fsdp", n_shard, 2)
    (x_all, normed, query, keyval, mixed, mid, normed_mid, cosine, sine, gains, wq_full, wkv_full, wo_full) = call(
        functools.partial(attn_forward_kernel, n_shard),
        [idx_late] + packs,
        (
            shape((group_rows, model), BF16),
            shape((group_rows, model), BF16),
            shape((group_rows, QW), BF16),
            shape((group_rows, kv_width), BF16),
            shape((group_rows, QW), BF16),
            shape((group_rows, model), F32),
            shape((group_rows, model), BF16),
            shape((group_rows, 128), F32),
            shape((group_rows, 128), F32),
            shape((16, model), F32),
            shape((model, QW), BF16),
            shape((model, kv_width), BF16),
            shape((QW, model), BF16),
        ),
        [
            pltpu.VMEM((group_rows, QW), F32),
            pltpu.VMEM((group_rows, kv_width), F32),
            pltpu.VMEM((n_shard, pack_rows, model), BF16),
            pltpu.VMEM((n_shard, 16, model), BF16),
            pltpu.SemaphoreType.DMA((6,)),
            pltpu.SemaphoreType.DMA((n_shard,)),
            pltpu.SemaphoreType.DMA((n_shard,)),
        ],
        micros=MICROS[0],
        raw=range(1, 7),
    )
    middle = n_rep // 2
    chunk = ff // n_shard
    slab_rows = width * 4 // n_rep
    a_rows = 3 * width + 16
    a_slab = (a_rows // n_rep, model)
    gu_beside = [exchange(piece, "fsdp", n_shard, 1) for piece in (w_gateup[0], direct_one, direct_two)]
    cot_own, down_own, cot_across, down_across, around_one, around_two, _ = lax.optimization_barrier(
        (cotangent, w_down[0].T, cot_across, down_across, around_one, around_two, gains)
    )
    around_beside = [exchange(piece, "fsdp", n_shard, 1) for piece in (around_one, around_two)]
    gu = [w_gateup[0], gu_beside[0], direct_one, direct_two, around_one, around_two] + gu_beside[1:] + around_beside
    cot = [cot_own, exchange(cot_own, "fsdp", n_shard, 1), cot_across, exchange(cot_across, "fsdp", n_shard, 1)]
    down_beside = exchange(down_own, "fsdp", n_shard, 1)
    half_act, half_dn, one_lo, one_hi, dcot, gu_full, own_mid = call(
        functools.partial(mlp_kernel, n_shard, n_rep, True),
        [idx, normed_mid, mid, down_own, down_beside] + cot + gu,
        (
            shape((row_count, model), F32),
            shape((group_rows, model), F32),
            shape((middle, 2 * slab_rows, chunk), BF16),
            shape((middle, 2 * slab_rows, chunk), BF16),
            shape((group_rows, model), BF16),
            shape((model, 2 * ff), BF16),
            shape((group_rows, width), BF16),
        ),
        [
            pltpu.VMEM((n_rep, 2 * slab_rows, chunk), BF16),
            pltpu.VMEM((model, 2 * chunk), BF16),
            pltpu.VMEM((group_rows, 2 * chunk), BF16),
            pltpu.SemaphoreType.DMA((10,)),
            pltpu.SemaphoreType.DMA((2,)),
            pltpu.SemaphoreType.DMA((n_shard,)),
        ],
        micros=MICROS[1],
        raw=range(3, 15 + n_shard),
    )
    down_across, _ = lax.optimization_barrier((down_across, half_act))
    down_corner = exchange(down_across, "fsdp", n_shard, 1)
    out_act, d_normed_mid, two_lo, two_hi = call(
        functools.partial(mlp_kernel, n_shard, n_rep, False),
        [idx, normed_mid, half_act, down_across, down_corner, dcot, gu_full, own_mid, half_dn],
        (
            shape((model, row_count), F32),
            shape((group_rows, model), F32),
            shape((middle, slab_rows, chunk), BF16),
            shape((middle, slab_rows, chunk), BF16),
        ),
        [
            pltpu.VMEM((n_rep, slab_rows, chunk), BF16),
            pltpu.VMEM((model, 2 * chunk), BF16),
            pltpu.SemaphoreType.DMA((2,)),
        ],
        micros=MICROS[2],
        raw=(3, 4),
    )
    one = replica_steps(one_lo, one_hi, n_rep, TURNED[0])
    two = replica_steps(two_lo, two_hi, n_rep, TURNED[1])
    d_attn, d_mixed, d_mid, part_out, part_gain = call(
        functools.partial(residual_backward_kernel, n_shard),
        [idx, mid, d_normed_mid, dcot, mixed, gains, wo_full],
        (
            shape((group_rows, model), BF16),
            shape((group_rows, QW), BF16),
            shape((row_count, model), F32),
            shape((width, model), F32),
            shape((8, model), F32),
        ),
        micros=MICROS[3],
    )
    reached = [0, 0]
    results = {}

    def advance(kernel):
        for chain, steps in enumerate((one, two)):
            while reached[chain] < TIES[kernel][chain]:
                results[chain] = next(steps)
                reached[chain] += 1
        return [results[chain] for chain in results]

    halves = []
    for first_row in (0, group_rows // 2):
        d_mixed = after(d_mixed, *advance(len(halves)), *(half[0] for half in halves))
        halves.append(
            call(
                functools.partial(heads_backward_kernel, first_row),
                [idx, query, keyval, d_mixed, cosine, sine],
                (shape((group_rows // 2, QW), BF16), shape((group_rows // 2, kv_width), BF16)),
                micros=MICROS[4],
            )
        )
    d_mid = after(d_mid, *advance(2))
    in_grad, a_lo, a_hi = call(
        functools.partial(input_backward_kernel, n_shard, n_rep),
        [idx, x_all, normed, gains, wq_full, wkv_full, d_mid, part_out, part_gain,
         halves[0][0], halves[1][0], halves[0][1], halves[1][1]],
        (
            shape((model, row_count), F32),
            shape((middle,) + a_slab, BF16),
            shape((middle,) + a_slab, BF16),
        ),
        [
            pltpu.VMEM((a_rows, model), F32),
            pltpu.VMEM((group_rows, QW), BF16),
            pltpu.VMEM((group_rows, kv_width), BF16),
        ],
        micros=MICROS[5],
    )
    one, two = last_of(one), last_of(two)
    attn = last_of(replica_steps(a_lo, a_hi, n_rep, TURNED[2]))
    grad_down = call(
        functools.partial(unpack_down_kernel, n_rep),
        [idx] + list(one),
        shape((model, chunk), F32),
        micros=1,
    )
    grad_gateup = call(
        functools.partial(unpack_mlp_kernel, n_rep, n_shard),
        [idx] + list(one) + list(two),
        shape((width, 2 * ff), F32),
        micros=2,
    )
    grad_query, grad_keyval, grad_out, own_gain_attn, own_gain_mlp = call(
        functools.partial(unpack_attn_kernel, n_rep),
        [idx] + list(attn),
        (
            shape((width, model), F32),
            shape((width, kv_width), F32),
            shape((width, model), F32),
            shape((1, width), F32),
            shape((1, width), F32),
        ),
        [pltpu.VMEM((a_rows, model), F32)],
        micros=2,
    )
    return (
        out_act.T,
        in_grad.T,
        grad_query[None],
        grad_keyval[None],
        grad_out[None],
        grad_gateup[None],
        grad_down.T[None],
        own_gain_attn,
        own_gain_mlp,
    )


def solution(mesh):
    placed = (
        P(("rep", "fsdp"), None),
        P(("rep", "fsdp")),
        P(("rep", "fsdp")),
        P(None, "fsdp", None),
        P(None, "fsdp", None),
        P(None, "fsdp", None),
        P(None, "fsdp", None),
        P(None, "fsdp", None),
        P(None, "fsdp"),
        P(None, "fsdp"),
        P(("rep", "fsdp"), None),
    )
    return jax.shard_map(
        functools.partial(on_device, mesh.shape["rep"], mesh.shape["fsdp"]),
        mesh=mesh,
        in_specs=placed,
        out_specs=(
            P(("rep", "fsdp"), None),
            P(("rep", "fsdp"), None),
            P(None, "fsdp", None),
            P(None, "fsdp", None),
            P(None, "fsdp", None),
            P(None, "fsdp", None),
            P(None, "fsdp", None),
            P(None, "fsdp"),
            P(None, "fsdp"),
        ),
        check_vma=False,
    )
```
